256 devices in a mesh: seq: 64 (over z, x_lo, y), head: 4 (over x_hi, core).
Axes of the slice: x: 4 (x_hi: 2, x_lo: 2; x = x_hi * 2 + x_lo), y: 4, z: 8, core: 2. Of those that a mesh axis runs over, the one named last changes fastest.
Arguments:
- tokens: bfloat16 [65536, 2048], P('seq', 'head'), may hold values from -20 to 20
- w_query: bfloat16 [2048, 2048], P(None, 'head'), may hold values from -1 to 1
- w_key: bfloat16 [2048, 2048], P(None, 'head'), may hold values from -1 to 1
- w_value: bfloat16 [2048, 2048], P(None, 'head'), may hold values from -0.125 to 0.125
- w_out: bfloat16 [2048, 2048], P('head'), may hold values from -0.125 to 0.125
Outputs:
- attended: bfloat16 [65536, 2048], P(('seq', 'head'))
The draws below stay inside these ranges and needn't reach their ends.
All inputs are finite; a program needn't handle non-finite values.
Results may differ from the reference program's by a relative error of at most 0.04.
Values may be sent and summed in bfloat16 or wider, within the bound.
A program may use at most 128 MiB of HBM per device.

```python
import math
import jax
import jax.numpy as jnp
from jax import lax

D = 2048
H = 16
DH = 128
STRIDE = 256
TOKENS = 65536
ROWS = 256
N_HEAD = 4


def draw_tokens(key, part):
    drawn = jax.random.normal(jax.random.fold_in(key, 1), (TOKENS, D), jnp.float32)
    return jnp.clip(drawn, -6.0, 6.0).astype(jnp.bfloat16)


def paired_normals(key):
    first = jnp.clip(jax.random.normal(jax.random.fold_in(key, 11), (D, D), jnp.float32), -6.0, 6.0)
    second = jnp.clip(jax.random.normal(jax.random.fold_in(key, 12), (D, D), jnp.float32), -6.0, 6.0)
    return (first, second)


def draw_w_query(key, part):
    first, second = paired_normals(key)
    return jnp.clip(first * (1.6 / math.sqrt(D)), -0.2, 0.2).astype(jnp.bfloat16)


def draw_w_key(key, part):
    first, second = paired_normals(key)
    blended = second
    return jnp.clip(blended * (1.6 / math.sqrt(D)), -0.3, 0.3).astype(jnp.bfloat16)


def steps_of(stream_key, shape, shards, low, top_value):
    level, own = 1.0, jax.random.fold_in(stream_key, 6)
    for dim, parts in shards:
        steps = jnp.exp(jax.random.uniform(jax.random.fold_in(own, dim), (parts,), jnp.float32, low / len(shards), top_value / len(shards)))
        level = level * jnp.repeat(steps, shape[dim] // parts).reshape([-1 if axis == dim else 1 for axis in range(len(shape))])
    return level


def noise(rng, extent, width, bound, cuts=(), kind=jnp.bfloat16):
    entries = width * jax.random.normal(rng, extent, jnp.float32)
    if cuts:
        entries = entries * steps_of(rng, extent, cuts, -0.22, 0.18)
    return jnp.clip(entries, -bound, bound).astype(kind)


def setup_inputs(seed: int = 0) -> dict:
    key_of = jax.random.split(jax.random.key(seed), 6)
    return {
        "tokens": draw_tokens(jax.random.fold_in(key_of[5], 71), 0),
        "w_query": draw_w_query(jax.random.fold_in(key_of[5], 71), 0),
        "w_key": draw_w_key(jax.random.fold_in(key_of[5], 71), 0),
        "w_value": noise(key_of[3], (D, D), D ** -0.5, 0.125, ((1, 4),)),
        "w_out": noise(key_of[4], (D, D), D ** -0.5, 0.125, ((0, 4),)),
    }


def local_part(query_one, key_one, value_one):
    score_scale = DH ** -0.5
    query_rows = query_one.reshape(ROWS, STRIDE, DH).astype(jnp.float32)
    key_rows = key_one.reshape(ROWS, STRIDE, DH)
    value_rows = value_one.reshape(ROWS, STRIDE, DH)
    padding = jnp.zeros((1, STRIDE, DH), key_one.dtype)
    key_window = jnp.concatenate([jnp.concatenate([padding, key_rows[:-1]], 0), key_rows], 1).astype(jnp.float32)
    value_window = jnp.concatenate([jnp.concatenate([padding, value_rows[:-1]], 0), value_rows], 1).astype(jnp.float32)
    scores = jnp.einsum('rtd,rud->rtu', query_rows, key_window) * score_scale
    query_index = jnp.arange(STRIDE)[None, :, None]
    key_index = jnp.arange(2 * STRIDE)[None, None, :]
    row_index = jnp.arange(ROWS)[:, None, None]
    allowed = (key_index > query_index) & (key_index <= query_index + STRIDE) & (row_index * STRIDE + key_index - STRIDE >= 0)
    top_score = jnp.max(jnp.where(allowed, scores, -1e30), axis=-1)
    prob_weights = jnp.where(allowed, jnp.exp(scores - top_score[..., None]), 0.0)
    total_weight = jnp.sum(prob_weights, axis=-1)
    rounded = prob_weights.astype(jnp.bfloat16).astype(jnp.float32)
    result = jnp.einsum('rtu,rud->rtd', rounded, value_window)
    return result.reshape(TOKENS, DH), top_score.reshape(TOKENS), total_weight.reshape(TOKENS)


def column_part(query_one, key_one, value_one):
    score_scale = DH ** -0.5
    query_rows = query_one.reshape(ROWS, STRIDE, DH).astype(jnp.float32)
    key_rows = key_one.reshape(ROWS, STRIDE, DH).astype(jnp.float32)
    value_rows = value_one.reshape(ROWS, STRIDE, DH).astype(jnp.float32)
    scores = jnp.einsum('rcd,scd->crs', query_rows, key_rows) * score_scale
    allowed = jnp.arange(ROWS)[None, :, None] > jnp.arange(ROWS)[None, None, :]
    top_score = jnp.max(jnp.where(allowed, scores, -1e30), axis=-1)
    prob_weights = jnp.where(allowed, jnp.exp(scores - top_score[..., None]), 0.0)
    total_weight = jnp.sum(prob_weights, axis=-1)
    rounded = prob_weights.astype(jnp.bfloat16).astype(jnp.float32)
    summed = jnp.einsum('crs,scd->rcd', rounded, value_rows)
    result = (summed / jnp.maximum(total_weight.T, 1.0)[..., None]).astype(jnp.bfloat16)
    return result.reshape(TOKENS, DH), top_score.T.reshape(TOKENS), total_weight.T.reshape(TOKENS)


def attend_head(pieces):
    query_one, key_one, value_one = pieces
    local_out, local_top, local_total = local_part(query_one, key_one, value_one)
    column_out, column_top, column_total = column_part(query_one, key_one, value_one)
    top_score = jnp.maximum(local_top, column_top)
    local_weight = jnp.exp(local_top - top_score)
    column_weight = column_total * jnp.exp(column_top - top_score)
    denominator = local_total * local_weight + column_weight
    mixed = (local_out * local_weight[:, None] + column_out.astype(jnp.float32) * column_weight[:, None]) / denominator[:, None]
    return mixed.astype(jnp.bfloat16)


def reference(tokens, w_query, w_key, w_value, w_out):
    query = jnp.dot(tokens, w_query, preferred_element_type=jnp.float32).astype(jnp.bfloat16)
    key_all = jnp.dot(tokens, w_key, preferred_element_type=jnp.float32).astype(jnp.bfloat16)
    value = jnp.dot(tokens, w_value, preferred_element_type=jnp.float32).astype(jnp.bfloat16)
    query_heads = query.reshape(TOKENS, H, DH).transpose(1, 0, 2)
    key_heads = key_all.reshape(TOKENS, H, DH).transpose(1, 0, 2)
    value_heads = value.reshape(TOKENS, H, DH).transpose(1, 0, 2)
    mixed = lax.map(attend_head, (query_heads, key_heads, value_heads))
    mixed = mixed.transpose(1, 0, 2).reshape(TOKENS, D)
    group_width = D // N_HEAD
    running = jnp.zeros((TOKENS, D), jnp.float32)
    for group in range(N_HEAD):
        group_term = jnp.dot(mixed[:, group * group_width:(group + 1) * group_width], w_out[group * group_width:(group + 1) * group_width], preferred_element_type=jnp.float32).astype(jnp.bfloat16)
        group_term = lax.optimization_barrier(group_term)
        running = running + group_term.astype(jnp.float32)
    return running.astype(jnp.bfloat16)
```

```python
import functools
import math

import jax
import jax.numpy as jnp
from jax import lax
from jax.experimental import pallas as pl
from jax.experimental.pallas import tpu as pltpu
from jax.sharding import PartitionSpec as P

MESH = pl.DeviceIdType.MESH
BF16 = jnp.bfloat16
F32 = jnp.float32
DH = 128
HEADS = 4
T = 1024
F = 512
BLK = 256
PIECE = 16
SEND = F + DH
SCALE2 = DH ** (-0.5) * math.log2(math.e)
NEG = -1e30


def dot(a, b):
    return jnp.dot(a, b, preferred_element_type=F32)


def dot_t(a, b):
    return lax.dot_general(a, b, (((1,), (1,)), ((), ())), preferred_element_type=F32)


def ds(start, size):
    return pl.ds(pl.multiple_of(start, size), size)


def iota(shape, dim):
    return lax.broadcasted_iota(jnp.int32, shape, dim)


def three_parts(value):
    parts = []
    for _ in range(3):
        part = value.astype(BF16).astype(F32)
        parts.append(part)
        value = value - part
    return parts


def kernel(
    tok, wq, wk, wv, wo, out,
    row_tok, class_tok, perm, arrived, w_in, w_o, row_acc, class_acc, qkv,
    col_f, col, ret, loc, loc_stat, send_mix, mix,
    load_sem, ag_s, ag_r, a2a_s, a2a_r, x_s, x_r, fwd_s, fwd_r, halo_s, halo_r,
    ret_s, ret_r, wo_s, wo_r, mix_s, mix_r,
):
    seq, h = lax.axis_index("seq"), lax.axis_index("head")
    n_seq = lax.axis_size("seq")
    hi, core = h // 2, h % 2
    z, x_lo, y = seq // 8, (seq // 4) % 2, seq % 4
    g = z * 4 + y
    groups = n_seq // 2
    half = (hi + x_lo) % 2
    other_seq = z * 8 + (1 - x_lo) * 4 + y
    sib = hi * 2 + 1 - core
    far = (1 - hi) * 2 + core

    def remote(src, dst, s_sem, r_sem, **device):
        return pltpu.make_async_remote_copy(
            src_ref=src, dst_ref=dst, send_sem=s_sem, recv_sem=r_sem,
            device_id=device, device_id_type=MESH,
        )

    def seq_of(group, x):
        return (group // 4) * 8 + x * 4 + group % 4

    barrier = pltpu.get_barrier_semaphore()

    def greet(k, carry):
        pl.semaphore_signal(
            barrier, inc=1, device_id={"seq": (seq + k) % n_seq}, device_id_type=MESH
        )
        return carry

    lax.fori_loop(1, n_seq, greet, 0)
    pl.semaphore_signal(barrier, inc=1, device_id={"head": sib}, device_id_type=MESH)
    for k in range(2):
        pl.semaphore_signal(
            barrier, inc=1, device_id={"head": (1 - hi) * 2 + k}, device_id_type=MESH
        )
    pl.semaphore_signal(
        barrier, inc=1, device_id={"seq": other_seq, "head": far}, device_id_type=MESH
    )

    own_lanes = ds(core * F, F)
    loads = [
        pltpu.make_async_copy(w, w_in.at[i], load_sem.at[i])
        for i, w in enumerate((wq, wk, wv))
    ]
    loads.append(pltpu.make_async_copy(wo, w_o.at[ds(h * F, F)], load_sem.at[3]))
    loads.append(pltpu.make_async_copy(tok, row_tok.at[hi, :, own_lanes], load_sem.at[4]))
    for load in loads:
        load.start()

    def permute(i, carry):
        j = iota((BLK, 1), 0)
        source = (
            ((j // 4) % 4) * BLK + ((i % 2) * 16 + j // 16) * 8 + (i // 2) * 4 + j % 4
        )
        pick = jnp.where(iota((BLK, T), 1) == source, 1.0, 0.0).astype(BF16)
        perm[i // 2, ds((i % 2) * BLK, BLK), :] = dot(pick, tok[...]).astype(BF16)
        return carry

    lax.fori_loop(0, 4, permute, 0)
    keep = pltpu.make_async_copy(
        perm.at[:, ds(g * PIECE, PIECE)], arrived.at[:, ds(g * PIECE, PIECE)], load_sem.at[5]
    )
    keep.start()

    pl.semaphore_wait(barrier, n_seq - 1 + 4)

    ag_far = remote(tok, row_tok.at[hi, :, own_lanes], ag_s.at[0], ag_r.at[0], head=far)
    ag_sib = remote(tok, row_tok.at[hi, :, own_lanes], ag_s.at[1], ag_r.at[1], head=sib)
    ag_far_block = row_tok.at[1 - hi, :, own_lanes]
    ag_fwd = remote(ag_far_block, ag_far_block, ag_s.at[2], ag_r.at[2], head=sib)

    def scatter(k, carry):
        to = (g + k) % groups
        remote(
            perm.at[:, ds(to * PIECE, PIECE)], arrived.at[:, ds(g * PIECE, PIECE)],
            a2a_s.at[0], a2a_r.at[0], seq=seq_of(to, x_lo),
        ).start()
        return carry

    lax.fori_loop(1, groups, scatter, 0)
    ag_far.start()
    ag_sib.start()

    def project(source, rows_of, write):
        def step(i, carry):
            n, b = i % 3, 3 - i // 3
            rows = ds(b * BLK, BLK)
            res = dot(source[rows, :], w_in[n, rows_of, :])
            for k in range(HEADS):
                write(n * HEADS + k, b, rows, res[:, k * DH : (k + 1) * DH])
            return carry

        return step

    def row_first(k, b, rows, res):
        row_acc[k, rows, :] = res

    def row_last(k, b, rows, res):
        qkv[k, ds((b + 1) * BLK, BLK), :] = (row_acc[k, rows, :] + res).astype(BF16)

    def class_first(k, b, rows, res):
        class_acc[k, rows, :] = res

    def class_last(k, b, rows, res):
        class_acc[k, rows, :] = class_acc[k, rows, :] + res

    own_rows, far_rows = ds(hi * 2 * F, 2 * F), ds((1 - hi) * 2 * F, 2 * F)
    for i in (0, 1, 2, 4):
        loads[i].wait()
    ag_sib.wait_recv()
    lax.fori_loop(0, 12, project(row_tok.at[hi], own_rows, row_first), 0)

    keep.wait()
    got = arrived.at[:, pl.ds(0, (groups - 1) * PIECE)]
    pltpu.make_async_copy(got, got, a2a_r.at[0]).wait()
    mine = lambda x: class_tok.at[hi, ds(x * F, F), own_lanes]
    theirs = lambda x: class_tok.at[1 - hi, ds(x * F, F), own_lanes]
    to_cross = remote(
        arrived.at[half], mine(x_lo), x_s.at[0], x_r.at[0], seq=other_seq, head=far
    )
    to_pair = remote(
        arrived.at[1 - half], mine(x_lo), x_s.at[1], x_r.at[1], seq=other_seq, head=h
    )
    to_far = remote(arrived.at[1 - half], mine(x_lo), x_s.at[2], x_r.at[2], seq=seq, head=far)
    to_sib = remote(arrived.at[half], mine(x_lo), x_s.at[3], x_r.at[3], seq=seq, head=sib)
    for copy in (to_far, to_cross, to_pair, to_sib):
        copy.start()
    stay = pltpu.make_async_copy(arrived.at[half], mine(x_lo), load_sem.at[6])
    stay.start()

    ag_far.wait_recv()
    ag_fwd.start()
    ag_fwd.wait_recv()
    lax.fori_loop(0, 12, project(row_tok.at[1 - hi], far_rows, row_last), 0)
    halo = remote(
        qkv.at[pl.ds(HEADS, 2 * HEADS), pl.ds(T, BLK)],
        qkv.at[pl.ds(HEADS, 2 * HEADS), pl.ds(0, BLK)],
        halo_s.at[0], halo_r.at[0], seq=(seq + 1) % n_seq,
    )
    halo.start()

    forwards = []
    for i, (copy, block) in enumerate(
        (
            (to_pair, mine(1 - x_lo)),
            (to_cross, theirs(1 - x_lo)),
            (to_far, theirs(x_lo)),
        )
    ):
        copy.wait_recv()
        forward = remote(block, block, fwd_s.at[i], fwd_r.at[i], head=sib)
        forward.start()
        forwards.append(forward)
    wo_mine = w_o.at[ds(h * F, F)]
    wo_theirs = w_o.at[ds(far * F, F)]
    wo_far = remote(wo, wo_mine, wo_s.at[0], wo_r.at[0], seq=other_seq, head=far)
    wo_sib = remote(wo, wo_mine, wo_s.at[1], wo_r.at[1], head=sib)
    wo_fwd = remote(wo_theirs, wo_theirs, wo_s.at[2], wo_r.at[2], head=sib)
    wo_far.start()
    wo_sib.start()

    to_sib.wait_recv()
    stay.wait()
    forwards[0].wait_recv()
    lax.fori_loop(0, 12, project(class_tok.at[hi], own_rows, class_first), 0)
    forwards[1].wait_recv()
    forwards[2].wait_recv()
    lax.fori_loop(0, 12, project(class_tok.at[1 - hi], far_rows, class_last), 0)

    def row_of(n):
        return ((n % 128) // 16) * 32 + (n // 128) * 16 + n % 16

    earlier = row_of(iota((BLK, BLK), 0)) > row_of(iota((BLK, BLK), 1))
    lane = iota((BLK, DH), 1)
    col_f[HEADS] = jnp.zeros((T, DH), F32)

    def column(k, carry):
        for c in range(4):
            at = pl.ds(c, BLK, stride=4)
            query = class_acc[k, at, :].astype(BF16)
            key = class_acc[HEADS + k, at, :].astype(BF16)
            value = class_acc[2 * HEADS + k, at, :].astype(BF16)
            scores = jnp.where(earlier, dot_t(query, key), NEG)
            top = jnp.max(scores, axis=1, keepdims=True)
            weights = jnp.where(earlier, jnp.exp2((scores - top) * SCALE2), 0.0)
            total = jnp.sum(weights, axis=1, keepdims=True)
            summed = dot(weights.astype(BF16), value)
            col_f[k, at, :] = summed * (1.0 / jnp.maximum(total, 1.0))
            stat = col_f[HEADS, at, :]
            for i, part in enumerate(three_parts(top * SCALE2) + three_parts(total)):
                stat = jnp.where(lane == k * 8 + i, part, stat)
            col_f[HEADS, at, :] = stat
        return carry

    lax.fori_loop(0, HEADS, column, 0)
    for k in range(HEADS + 1):
        col[:, k * DH : (k + 1) * DH] = col_f[k].astype(BF16)

    slot = ds((g * 2 + half) * PIECE, PIECE)

    def give_back(k, carry):
        to = (seq + k) % n_seq
        piece = ((to // 4) % 2) * F + ((to // 8) * 4 + to % 4) * PIECE
        remote(
            col.at[ds(piece, PIECE)], ret.at[slot], ret_s.at[0], ret_r.at[0], seq=to
        ).start()
        return carry

    lax.fori_loop(1, n_seq, give_back, 0)
    own_ret = pltpu.make_async_copy(
        col.at[ds(x_lo * F + g * PIECE, PIECE)], ret.at[slot], load_sem.at[7]
    )
    own_ret.start()

    halo.wait_recv()
    lower = iota((BLK, BLK), 1) <= iota((BLK, BLK), 0)

    def local(b, carry):
        before = jnp.where(jnp.logical_and(seq == 0, b == 0), NEG, 0.0)
        prev, cur = ds(b * BLK, BLK), ds((b + 1) * BLK, BLK)
        for k in range(HEADS):
            query = qkv[k, cur, :]
            s_cur = dot_t(query, qkv[HEADS + k, cur, :])
            s_prev = dot_t(query, qkv[HEADS + k, prev, :]) + before
            scores = jnp.where(lower, s_cur, s_prev)
            top = jnp.max(scores, axis=1, keepdims=True)
            weights = jnp.exp2((scores - top) * SCALE2)
            total = jnp.sum(weights, axis=1, keepdims=True)
            loc[k, prev, :] = dot(
                jnp.where(lower, weights, 0.0).astype(BF16), qkv[2 * HEADS + k, cur, :]
            ) + dot(
                jnp.where(lower, 0.0, weights).astype(BF16), qkv[2 * HEADS + k, prev, :]
            )
            loc_stat[k, prev, :] = top * SCALE2
            loc_stat[HEADS + k, prev, :] = total
        return carry

    lax.fori_loop(0, 4, local, 0)

    wo_far.wait_recv()
    wo_fwd.start()
    own_ret.wait()
    back = ret.at[pl.ds(0, (n_seq - 1) * PIECE)]
    pltpu.make_async_copy(back, back, ret_r.at[0]).wait()

    def merge(i, carry):
        b = ((hi + 1 - i // 2) % 2) * 2 + (core + (i + 1) // 2) % 2
        j = iota((BLK, 1), 0)
        source = (j // 4) * PIECE + b * 4 + j % 4
        pick = jnp.where(iota((BLK, T), 1) == source, 1.0, 0.0).astype(BF16)
        rows = ds(b * BLK, BLK)
        results = dot(pick, ret[...])
        for k in range(HEADS):
            at = F + k * 8
            part = [results[:, at + m : at + m + 1] for m in range(6)]
            col_top = part[0] + part[1] + part[2]
            col_total = part[3] + part[4] + part[5]
            top = jnp.maximum(loc_stat[k, rows, :], col_top)
            local_weight = jnp.exp2(loc_stat[k, rows, :] - top)
            col_weight = col_total * jnp.exp2(col_top - top)
            inv = 1.0 / (loc_stat[HEADS + k, rows, :] * local_weight + col_weight)
            send_mix[i, :, k * DH : (k + 1) * DH] = (
                loc[k, rows, :] * (local_weight * inv)
                + results[:, k * DH : (k + 1) * DH] * (col_weight * inv)
            ).astype(BF16)

        @pl.when(i < 3)
        def _():
            remote(
                send_mix.at[i], mix.at[hi, :, own_lanes], mix_s.at[i], mix_r.at[i], head=b
            ).start()

        return carry

    lax.fori_loop(0, 4, merge, 0)
    mix[hi, :, own_lanes] = send_mix[3]

    def mix_copy(i, b):
        return remote(
            send_mix.at[i], mix.at[hi, :, own_lanes], mix_s.at[i], mix_r.at[i], head=b
        )

    mix_copies = [mix_copy(0, far), mix_copy(1, (1 - hi) * 2 + 1 - core), mix_copy(2, sib)]
    loads[3].wait()
    wo_sib.wait_recv()
    mix_copies[2].wait_recv()
    outs = 4

    def out_first(i, carry):
        cols = ds(i * F, F)
        res = dot(mix[hi], w_o[own_rows, cols])
        for k in range(HEADS):
            row_acc[k, ds(i * BLK, BLK), :] = res[:, k * DH : (k + 1) * DH]
        return carry

    lax.fori_loop(0, outs, out_first, 0)
    wo_fwd.wait_recv()
    mix_copies[0].wait_recv()
    mix_copies[1].wait_recv()

    def out_last(i, carry):
        cols = ds(i * F, F)
        res = dot(mix[1 - hi], w_o[far_rows, cols])
        so_far = jnp.concatenate(
            [row_acc[k, ds(i * BLK, BLK), :] for k in range(HEADS)], axis=1
        )
        out[:, cols] = (res + so_far).astype(BF16)
        return carry

    lax.fori_loop(0, outs, out_last, 0)

    sent = perm.at[:, pl.ds(0, (groups - 1) * PIECE)]
    pltpu.make_async_copy(sent, sent, a2a_s.at[0]).wait()
    pltpu.make_async_copy(back, back, ret_s.at[0]).wait()
    for copy in (
        [ag_far, ag_sib, ag_fwd, to_cross, to_pair, to_far, to_sib, halo]
        + forwards + [wo_far, wo_sib, wo_fwd] + mix_copies
    ):
        copy.wait_send()


def shards(tokens, w_query, w_key, w_value, w_out):
    vmem = pl.BlockSpec(memory_space=pltpu.VMEM)
    anywhere = pl.BlockSpec(memory_space=pl.ANY)
    dma = lambda n: pltpu.SemaphoreType.DMA((n,))
    d = 4 * F
    return pl.pallas_call(
        kernel,
        out_shape=jax.ShapeDtypeStruct((BLK, d), BF16),
        in_specs=[vmem] + [anywhere] * 4,
        out_specs=vmem,
        scratch_shapes=[
            pltpu.VMEM((2, T, 2 * F), BF16),
            pltpu.VMEM((2, T, 2 * F), BF16),
            pltpu.VMEM((2, T // 2, F), BF16),
            pltpu.VMEM((2, T // 2, F), BF16),
            pltpu.VMEM((3, d, F), BF16),
            pltpu.VMEM((d, d), BF16),
            pltpu.VMEM((12, T, DH), F32),
            pltpu.VMEM((12, T, DH), F32),
            pltpu.VMEM((12, T + BLK, DH), BF16),
            pltpu.VMEM((HEADS + 1, T, DH), F32),
            pltpu.VMEM((T, SEND), BF16),
            pltpu.VMEM((T, SEND), BF16),
            pltpu.VMEM((HEADS, T, DH), F32),
            pltpu.VMEM((2 * HEADS, T, 1), F32),
            pltpu.VMEM((4, BLK, F), BF16),
            pltpu.VMEM((2, BLK, 2 * F), BF16),
            dma(8), dma(3), dma(3), dma(1), dma(1), dma(4), dma(4), dma(3), dma(3),
            dma(1), dma(1), dma(1), dma(1), dma(3), dma(3), dma(3), dma(3),
        ],
        compiler_params=pltpu.CompilerParams(
            collective_id=0, has_side_effects=True, vmem_limit_bytes=62 << 20
        ),
    )(tokens, w_query, w_key, w_value, w_out)


def solution(mesh):
    in_specs = (
        P("seq", "head"),
        P(None, "head"),
        P(None, "head"),
        P(None, "head"),
        P("head", None),
    )
    out_specs = P(("seq", "head"), None)
    return jax.shard_map(shards, mesh=mesh, in_specs=in_specs, out_specs=out_specs, check_vma=False)
```

```python
import functools
import math

import jax
import jax.numpy as jnp
from jax import lax
from jax.experimental import pallas as pl
from jax.experimental.pallas import tpu as pltpu
from jax.sharding import PartitionSpec as P

MESH = pl.DeviceIdType.MESH
BF16 = jnp.bfloat16
F32 = jnp.float32
DH = 128
HEADS = 4
T = 1024
F = 512
BLK = 256
PIECE = 16
LOG2E = math.log2(math.e)
SCALE2 = DH ** (-0.5) * LOG2E
NEG = -1e30


def dot(a, b):
    return jnp.dot(a, b, preferred_element_type=F32)


def dot_t(a, b):
    return lax.dot_general(a, b, (((1,), (1,)), ((), ())), preferred_element_type=F32)


def ds(start, size):
    return pl.ds(pl.multiple_of(start, size), size)


def iota(shape, dim):
    return lax.broadcasted_iota(jnp.int32, shape, dim)


def three_parts(value):
    parts = []
    for _ in range(3):
        part = value.astype(BF16)
        parts.append(part)
        value = value - part.astype(F32)
    return parts


def select_dot(pick, value):
    return sum(dot(pick, part) for part in three_parts(value))


def one_hot(hit):
    return jnp.where(hit, 1.0, 0.0).astype(BF16)


def kernel(
    tok, wq, wk, wv, wo, out,
    row_tok, class_tok, perm, arrived, w_in, w_o, row_acc, class_acc, qkv,
    col_f, col, ret, col_stat, ret_stat, loc, loc_stat, send_mix, mix,
    load_sem, ag_s, ag_r, a2a_s, a2a_r, x_s, x_r, fwd_s, fwd_r, halo_s, halo_r,
    ret_s, ret_r, stat_s, stat_r, wo_s, wo_r, mix_s, mix_r,
):
    seq, h = lax.axis_index("seq"), lax.axis_index("head")
    n_seq = lax.axis_size("seq")
    hi, core = h // 2, h % 2
    z, x_lo, y = seq // 8, (seq // 4) % 2, seq % 4
    g = z * 4 + y
    groups = n_seq // 2
    other_seq = z * 8 + (1 - x_lo) * 4 + y
    sib = hi * 2 + 1 - core
    far = (1 - hi) * 2 + core
    far_sib = (1 - hi) * 2 + 1 - core

    def remote(src, dst, s_sem, r_sem, **device):
        return pltpu.make_async_remote_copy(
            src_ref=src, dst_ref=dst, send_sem=s_sem, recv_sem=r_sem,
            device_id=device, device_id_type=MESH,
        )

    def seq_of(group, x):
        return (group // 4) * 8 + x * 4 + group % 4

    def wait_for(ref, sem):
        pltpu.make_async_copy(ref, ref, sem).wait()

    barrier = pltpu.get_barrier_semaphore()

    def greet(k, carry):
        pl.semaphore_signal(
            barrier, inc=1, device_id={"seq": (seq + k) % n_seq}, device_id_type=MESH
        )
        return carry

    lax.fori_loop(1, n_seq, greet, 0)
    for peer in (sib, far, far_sib):
        pl.semaphore_signal(barrier, inc=1, device_id={"head": peer}, device_id_type=MESH)
    pl.semaphore_signal(
        barrier, inc=1, device_id={"seq": other_seq, "head": far}, device_id_type=MESH
    )

    own_lanes = ds(core * F, F)
    own_rows, far_rows = ds(hi * 2 * F, 2 * F), ds((1 - hi) * 2 * F, 2 * F)
    loads = [
        pltpu.make_async_copy(w, w_in.at[i], load_sem.at[i])
        for i, w in enumerate((wq, wk, wv))
    ]
    loads.append(pltpu.make_async_copy(wo, w_o.at[ds(h * F, F)], load_sem.at[3]))
    loads.append(pltpu.make_async_copy(tok, row_tok.at[hi, :, own_lanes], load_sem.at[4]))
    for load in loads:
        load.start()

    def permute(i, carry):
        j = iota((BLK, 1), 0)
        source = (
            ((j // 4) % 4) * BLK + ((i % 2) * 16 + j // 16) * 8 + (i // 2) * 4 + j % 4
        )
        pick = one_hot(iota((BLK, T), 1) == source)
        perm[i // 2, ds((i % 2) * BLK, BLK), :] = dot(pick, tok[...]).astype(BF16)
        return carry

    lax.fori_loop(0, 4, permute, 0)
    here = ds(g * PIECE, PIECE)
    keeps = [
        pltpu.make_async_copy(perm.at[x, here], arrived.at[i, here], load_sem.at[5 + i])
        for i, x in enumerate((x_lo, 1 - x_lo))
    ]
    for keep in keeps:
        keep.start()

    pl.semaphore_wait(barrier, n_seq - 1 + 4)

    def scatter(i, x):
        def send(k, carry):
            to = (g + k) % groups
            remote(
                perm.at[x, ds(to * PIECE, PIECE)], arrived.at[i, here],
                a2a_s.at[i], a2a_r.at[i], seq=seq_of(to, x_lo),
            ).start()
            return carry

        lax.fori_loop(1, groups, send, 0)

    def rows_to_far(i):
        rows = pl.ds((1 - i) * 2 * BLK, 2 * BLK)
        theirs = row_tok.at[1 - hi, rows, own_lanes]
        return (
            remote(tok.at[rows], row_tok.at[hi, rows, own_lanes], ag_s.at[i], ag_r.at[i], head=far),
            remote(theirs, theirs, ag_s.at[2 + i], ag_r.at[2 + i], head=sib),
        )

    ag_far, ag_fwd = zip(rows_to_far(0), rows_to_far(1))
    ag_sib = remote(tok, row_tok.at[hi, :, own_lanes], ag_s.at[4], ag_r.at[4], head=sib)
    quarter = T // 8

    def wo_quarter(of, which):
        return w_o.at[ds(of * F + which * quarter, quarter)]

    wo_far = remote(
        wo.at[ds(y * quarter, quarter)], wo_quarter(h, y), wo_s.at[0], wo_r.at[0],
        seq=other_seq, head=far,
    )
    wo_sib = remote(wo, w_o.at[ds(h * F, F)], wo_s.at[1], wo_r.at[1], head=sib)
    wo_spread = [
        remote(
            wo_quarter(far, y), wo_quarter(far, y), wo_s.at[2 + k], wo_r.at[2 + k],
            seq=seq - y + (y + k) % 4,
        )
        for k in range(1, 4)
    ]
    wo_theirs = w_o.at[ds(far * F, F)]
    wo_fwd = remote(wo_theirs, wo_theirs, wo_s.at[2], wo_r.at[2], head=sib)

    scatter(0, x_lo)
    ag_far[0].start()
    ag_sib.start()
    scatter(1, 1 - x_lo)
    wo_far.start()
    wo_sib.start()

    def project(source, rows_of, first_row, blocks, write, heads=(0, HEADS)):
        lo, hi_ = heads

        def step(i, carry):
            n, b = i % 3, blocks - 1 - i // 3
            rows = ds(first_row + b * BLK, BLK)
            res = dot(source[rows, :], w_in[n, rows_of, lo * DH : hi_ * DH])
            for k in range(lo, hi_):
                write(n * HEADS + k, rows, res[:, (k - lo) * DH : (k - lo + 1) * DH])
            return carry

        lax.fori_loop(0, 3 * blocks, step, 0)

    def row_first(k, rows, res):
        row_acc[k, rows, :] = res

    def row_last(k, rows, res):
        behind = ds(rows.start + BLK, BLK)
        qkv[k, behind, :] = (row_acc[k, rows, :] + res).astype(BF16)

    def class_first(k, rows, res):
        class_acc[k, rows, :] = res

    def class_last(k, rows, res):
        class_acc[k, rows, :] = class_acc[k, rows, :] + res

    for i in (0, 1, 2, 4):
        loads[i].wait()
    ag_sib.wait_recv()
    project(row_tok.at[hi], own_rows, 0, 4, row_first)

    def mine(x):
        return class_tok.at[hi, ds(x * F, F), own_lanes]

    def theirs(x):
        return class_tok.at[1 - hi, ds(x * F, F), own_lanes]

    to_far = remote(arrived.at[0], mine(x_lo), x_s.at[0], x_r.at[0], head=far)
    to_sib = remote(arrived.at[0], mine(x_lo), x_s.at[1], x_r.at[1], head=sib)
    to_pair = remote(arrived.at[1], mine(x_lo), x_s.at[2], x_r.at[2], seq=other_seq)
    to_cross = remote(
        arrived.at[1], mine(x_lo), x_s.at[3], x_r.at[3], seq=other_seq, head=far
    )
    stay = pltpu.make_async_copy(arrived.at[0], mine(x_lo), load_sem.at[7])

    def forward(i, block):
        return remote(block, block, fwd_s.at[i], fwd_r.at[i], head=sib)

    fwd_far, fwd_pair, fwd_cross = (
        forward(0, theirs(x_lo)), forward(1, mine(1 - x_lo)), forward(2, theirs(1 - x_lo))
    )

    pieces = pl.ds(0, (groups - 1) * PIECE)
    keeps[0].wait()
    wait_for(arrived.at[0, pieces], a2a_r.at[0])
    to_far.start()
    to_sib.start()
    stay.start()

    ag_far[0].wait_recv()
    ag_fwd[0].start()
    wo_far.wait_recv()
    for copy in wo_spread:
        copy.start()
    ag_fwd[0].wait_recv()

    keeps[1].wait()
    wait_for(arrived.at[1, pieces], a2a_r.at[1])
    to_cross.start()
    to_pair.start()

    project(row_tok.at[1 - hi], far_rows, 2 * BLK, 2, row_last)
    halo = remote(
        qkv.at[pl.ds(HEADS, 2 * HEADS), pl.ds(T, BLK)],
        qkv.at[pl.ds(HEADS, 2 * HEADS), pl.ds(0, BLK)],
        halo_s.at[0], halo_r.at[0], seq=(seq + 1) % n_seq,
    )
    to_far.wait_recv()
    fwd_far.start()
    to_sib.wait_recv()
    stay.wait()
    project(class_tok.at[hi], own_rows, x_lo * F, 2, class_first)
    fwd_far.wait_recv()
    project(class_tok.at[1 - hi], far_rows, x_lo * F, 2, class_last)

    to_pair.wait_recv()
    fwd_pair.start()
    to_cross.wait_recv()
    fwd_cross.start()
    ag_far[1].start()
    halo.start()
    fwd_pair.wait_recv()
    project(class_tok.at[hi], own_rows, (1 - x_lo) * F, 2, class_first)
    fwd_cross.wait_recv()

    def row_of(n):
        return ((n % 128) // 16) * 32 + (n // 128) * 16 + n % 16

    earlier = row_of(iota((BLK, BLK), 0)) > row_of(iota((BLK, BLK), 1))
    lane = iota((BLK, DH), 1)
    place = (iota((BLK, DH), 0) % 4) * 32
    slot = g * 2 + x_lo
    own_ret = []
    for pair in range(2):
        heads = (2 * pair, 2 * pair + 2)
        project(class_tok.at[1 - hi], far_rows, (1 - x_lo) * F, 2, class_last, heads)

        def column(k, stat):
            for c in range(4):
                at = pl.ds(c, BLK, stride=4)
                head = 2 * pair + k
                query = class_acc[head, at, :].astype(BF16)
                key = class_acc[HEADS + head, at, :].astype(BF16)
                value = class_acc[2 * HEADS + head, at, :].astype(BF16)
                scores = jnp.where(earlier, dot_t(query, key), NEG)
                top = jnp.max(scores, axis=1, keepdims=True)
                weights = jnp.where(earlier, jnp.exp2((scores - top) * SCALE2), 0.0)
                total = jnp.maximum(jnp.sum(weights, axis=1, keepdims=True), 1.0)
                col_f[k, at, :] = dot(weights.astype(BF16), value) * (1.0 / total)
                level = top * SCALE2 + jnp.log(total) * LOG2E
                stat = jnp.where(lane == place + c * 8 + k, level, stat)
            return stat

        stat = lax.fori_loop(0, 2, column, jnp.zeros((BLK, DH), F32))
        for k in range(2):
            col[pair, :, k * DH : (k + 1) * DH] = col_f[k].astype(BF16)
        gather4 = one_hot(iota((n_seq, BLK), 1) // 4 == iota((n_seq, BLK), 0))
        col_stat[pair, :, 0, :] = select_dot(gather4, stat)

        def copies(to):
            at = ((to // 4) % 2) * groups + (to // 8) * 4 + to % 4
            return (
                (col.at[pair, ds(at * PIECE, PIECE)], ret.at[pair, ds(slot * PIECE, PIECE)]),
                (col_stat.at[pair, at], ret_stat.at[pair, slot]),
            )

        def give_back(k, carry):
            to = (seq + k) % n_seq
            values, stats = copies(to)
            remote(*stats, stat_s.at[pair], stat_r.at[pair], seq=to).start()
            remote(*values, ret_s.at[pair], ret_r.at[pair], seq=to).start()
            return carry

        lax.fori_loop(1, n_seq, give_back, 0)
        for i, (src, dst) in enumerate(copies(seq)):
            own_ret.append(pltpu.make_async_copy(src, dst, load_sem.at[8 + 2 * pair + i]))
            own_ret[-1].start()

    ag_far[1].wait_recv()
    ag_fwd[1].start()
    ag_fwd[1].wait_recv()
    project(row_tok.at[1 - hi], far_rows, 0, 2, row_last)
    for copy in wo_spread:
        copy.wait_recv()
    wo_fwd.start()
    halo.wait_recv()
    lower = iota((BLK, BLK), 1) <= iota((BLK, BLK), 0)

    def local(i, carry):
        b = 3 - i
        before = jnp.where(jnp.logical_and(seq == 0, b == 0), NEG, 0.0)
        prev, cur = ds(b * BLK, BLK), ds((b + 1) * BLK, BLK)
        for k in range(HEADS):
            query = qkv[k, cur, :]
            s_cur = dot_t(query, qkv[HEADS + k, cur, :])
            s_prev = dot_t(query, qkv[HEADS + k, prev, :]) + before
            scores = jnp.where(lower, s_cur, s_prev)
            top = jnp.max(scores, axis=1, keepdims=True)
            weights = jnp.exp2((scores - top) * SCALE2)
            total = jnp.sum(weights, axis=1, keepdims=True)
            loc[k, prev, :] = dot(
                jnp.where(lower, weights, 0.0).astype(BF16), qkv[2 * HEADS + k, cur, :]
            ) + dot(
                jnp.where(lower, 0.0, weights).astype(BF16), qkv[2 * HEADS + k, prev, :]
            )
            loc_stat[k, prev, :] = top * SCALE2
            loc_stat[HEADS + k, prev, :] = total
        return carry

    lax.fori_loop(0, 4, local, 0)

    def mix_copy(pair, i, b):
        lanes = pl.ds(pl.multiple_of(core * F + pair * 2 * DH, 2 * DH), 2 * DH)
        return remote(
            send_mix.at[pair, i], mix.at[hi, :, lanes],
            mix_s.at[pair, i], mix_r.at[pair, i], head=b,
        )

    for pair in range(2):
        own_ret[2 * pair].wait()
        own_ret[2 * pair + 1].wait()
        wait_for(ret_stat.at[pair, pl.ds(0, n_seq - 1)], stat_r.at[pair])
        wait_for(ret.at[pair, pl.ds(0, (n_seq - 1) * PIECE)], ret_r.at[pair])
        levels = three_parts(ret_stat[pair, :, 0, :])

        def merge(i, carry):
            b = ((hi + 1 - i // 2) % 2) * 2 + (core + (i + 1) // 2) % 2
            j = iota((BLK, 1), 0)
            pick = one_hot(iota((BLK, T), 1) == (j // 4) * PIECE + b * 4 + j % 4)
            rows = ds(b * BLK, BLK)
            results = dot(pick, ret[pair])
            pick = one_hot(iota((BLK, n_seq), 1) == j // 4)
            spread = sum(dot(pick, part) for part in levels)
            for k in range(2):
                head = 2 * pair + k
                level = jnp.sum(
                    jnp.where(lane == (b * 4 + j % 4) * 8 + k, spread, 0.0),
                    axis=1, keepdims=True,
                )
                top = jnp.maximum(loc_stat[head, rows, :], level)
                local_weight = jnp.exp2(loc_stat[head, rows, :] - top)
                col_weight = jnp.exp2(level - top)
                inv = 1.0 / (loc_stat[HEADS + head, rows, :] * local_weight + col_weight)
                send_mix[pair, i, :, k * DH : (k + 1) * DH] = (
                    loc[head, rows, :] * (local_weight * inv)
                    + results[:, k * DH : (k + 1) * DH] * (col_weight * inv)
                ).astype(BF16)

            @pl.when(i < 3)
            def _():
                mix_copy(pair, i, b).start()

            return carry

        lax.fori_loop(0, 4, merge, 0)
        mix[hi, :, pl.ds(pl.multiple_of(core * F + pair * 2 * DH, 2 * DH), 2 * DH)] = (
            send_mix[pair, 3]
        )

    mix_copies = [
        mix_copy(pair, i, b) for pair in range(2) for i, b in enumerate((far, far_sib, sib))
    ]
    loads[3].wait()
    wo_sib.wait_recv()
    mix_copies[2].wait_recv()
    mix_copies[5].wait_recv()

    def out_first(i, carry):
        res = dot(mix[hi], w_o[own_rows, ds(i * F, F)])
        for k in range(HEADS):
            row_acc[k, ds(i * BLK, BLK), :] = res[:, k * DH : (k + 1) * DH]
        return carry

    lax.fori_loop(0, 4, out_first, 0)
    wo_fwd.wait_recv()
    for i in (0, 1, 3, 4):
        mix_copies[i].wait_recv()

    def out_last(i, carry):
        res = dot(mix[1 - hi], w_o[far_rows, ds(i * F, F)])
        so_far = jnp.concatenate(
            [row_acc[k, ds(i * BLK, BLK), :] for k in range(HEADS)], axis=1
        )
        out[:, ds(i * F, F)] = (res + so_far).astype(BF16)
        return carry

    lax.fori_loop(0, 4, out_last, 0)

    for i in range(2):
        wait_for(perm.at[i, pieces], a2a_s.at[i])
        wait_for(col.at[i, pl.ds(0, (n_seq - 1) * PIECE)], ret_s.at[i])
        wait_for(col_stat.at[i, pl.ds(0, n_seq - 1)], stat_s.at[i])
    for copy in (
        *ag_far, *ag_fwd, ag_sib, to_far, to_sib, to_pair, to_cross,
        fwd_far, fwd_pair, fwd_cross, halo, wo_far, wo_sib, *wo_spread, wo_fwd, *mix_copies,
    ):
        copy.wait_send()


def shards(tokens, w_query, w_key, w_value, w_out):
    vmem = pl.BlockSpec(memory_space=pltpu.VMEM)
    anywhere = pl.BlockSpec(memory_space=pl.ANY)
    dma = lambda n: pltpu.SemaphoreType.DMA((n,))
    d = 4 * F
    n_seq = lax.axis_size("seq")
    return pl.pallas_call(
        kernel,
        out_shape=jax.ShapeDtypeStruct((BLK, d), BF16),
        in_specs=[vmem] + [anywhere] * 4,
        out_specs=vmem,
        scratch_shapes=[
            pltpu.VMEM((2, T, 2 * F), BF16),
            pltpu.VMEM((2, T, 2 * F), BF16),
            pltpu.VMEM((2, T // 2, F), BF16),
            pltpu.VMEM((2, T // 2, F), BF16),
            pltpu.VMEM((3, d, F), BF16),
            pltpu.VMEM((d, d), BF16),
            pltpu.VMEM((12, T, DH), F32),
            pltpu.VMEM((12, T, DH), F32),
            pltpu.VMEM((12, T + BLK, DH), BF16),
            pltpu.VMEM((2, T, DH), F32),
            pltpu.VMEM((2, T, 2 * DH), BF16),
            pltpu.VMEM((2, T, 2 * DH), BF16),
            pltpu.VMEM((2, n_seq, 1, DH), F32),
            pltpu.VMEM((2, n_seq, 1, DH), F32),
            pltpu.VMEM((HEADS, T, DH), F32),
            pltpu.VMEM((2 * HEADS, T, 1), F32),
            pltpu.VMEM((2, 4, BLK, 2 * DH), BF16),
            pltpu.VMEM((2, BLK, 2 * F), BF16),
            dma(12), dma(5), dma(5), dma(2), dma(2), dma(4), dma(4), dma(3), dma(3),
            dma(1), dma(1), dma(2), dma(2), dma(2), dma(2), dma(6), dma(6),
            pltpu.SemaphoreType.DMA((2, 3)), pltpu.SemaphoreType.DMA((2, 3)),
        ],
        compiler_params=pltpu.CompilerParams(
            collective_id=0, has_side_effects=True, vmem_limit_bytes=62 << 20
        ),
    )(tokens, w_query, w_key, w_value, w_out)


def solution(mesh):
    in_specs = (
        P("seq", "head"),
        P(None, "head"),
        P(None, "head"),
        P(None, "head"),
        P("head", None),
    )
    out_specs = P(("seq", "head"), None)
    return jax.shard_map(shards, mesh=mesh, in_specs=in_specs, out_specs=out_specs, check_vma=False)
```

```python
import functools
import math

import jax
import jax.numpy as jnp
from jax import lax
from jax.experimental import pallas as pl
from jax.experimental.pallas import tpu as pltpu
from jax.sharding import PartitionSpec as P

MESH = pl.DeviceIdType.MESH
BF16 = jnp.bfloat16
F32 = jnp.float32
DH = 128
HEADS = 4
T = 1024
F = 512
BLK = 256
PIECE = 16
LOG2E = math.log2(math.e)
SCALE2 = DH ** (-0.5) * LOG2E
NEG = -1e30


def dot(a, b):
    return jnp.dot(a, b, preferred_element_type=F32)


def dot_t(a, b):
    return lax.dot_general(a, b, (((1,), (1,)), ((), ())), preferred_element_type=F32)


def ds(start, size):
    return pl.ds(pl.multiple_of(start, size), size)


def iota(shape, dim):
    return lax.broadcasted_iota(jnp.int32, shape, dim)


def three_parts(value):
    parts = []
    for _ in range(3):
        part = value.astype(BF16)
        parts.append(part)
        value = value - part.astype(F32)
    return parts


def select_dot(pick, value):
    return sum(dot(pick, part) for part in three_parts(value))


def one_hot(hit):
    return jnp.where(hit, 1.0, 0.0).astype(BF16)


def kernel(
    tok, wq, wk, wv, wo, out,
    row_tok, class_tok, perm, arrived, w_in, w_o, row_acc, class_acc, qkv,
    col_f, col, ret, col_stat, ret_stat, loc, loc_stat, send_mix, mix,
    load_sem, ag_s, ag_r, a2a_s, a2a_r, x_s, x_r, fwd_s, fwd_r, halo_s, halo_r,
    ret_s, ret_r, stat_s, stat_r, wo_s, wo_r, mix_s, mix_r,
):
    seq, h = lax.axis_index("seq"), lax.axis_index("head")
    n_seq = lax.axis_size("seq")
    hi, core = h // 2, h % 2
    z, x_lo, y = seq // 8, (seq // 4) % 2, seq % 4
    g = z * 4 + y
    groups = n_seq // 2
    other_seq = z * 8 + (1 - x_lo) * 4 + y
    sib = hi * 2 + 1 - core
    far = (1 - hi) * 2 + core
    far_sib = (1 - hi) * 2 + 1 - core

    def remote(src, dst, s_sem, r_sem, **device):
        return pltpu.make_async_remote_copy(
            src_ref=src, dst_ref=dst, send_sem=s_sem, recv_sem=r_sem,
            device_id=device, device_id_type=MESH,
        )

    def seq_of(group, x):
        return (group // 4) * 8 + x * 4 + group % 4

    def wait_for(ref, sem):
        pltpu.make_async_copy(ref, ref, sem).wait()

    barrier = pltpu.get_barrier_semaphore()

    def greet(k, carry):
        pl.semaphore_signal(
            barrier, inc=1, device_id={"seq": (seq + k) % n_seq}, device_id_type=MESH
        )
        return carry

    lax.fori_loop(1, n_seq, greet, 0)
    for peer in (sib, far, far_sib):
        pl.semaphore_signal(barrier, inc=1, device_id={"head": peer}, device_id_type=MESH)
    pl.semaphore_signal(
        barrier, inc=1, device_id={"seq": other_seq, "head": far}, device_id_type=MESH
    )

    own_lanes = ds(core * F, F)
    own_rows, far_rows = ds(hi * 2 * F, 2 * F), ds((1 - hi) * 2 * F, 2 * F)
    loads = [
        pltpu.make_async_copy(w, w_in.at[i], load_sem.at[i])
        for i, w in enumerate((wq, wk, wv))
    ]
    loads.append(pltpu.make_async_copy(wo, w_o.at[ds(h * F, F)], load_sem.at[3]))
    loads.append(pltpu.make_async_copy(tok, row_tok.at[hi, :, own_lanes], load_sem.at[4]))
    for load in loads:
        load.start()

    def permute(i, carry):
        j = iota((BLK, 1), 0)
        source = (
            ((j // 4) % 4) * BLK + ((i % 2) * 16 + j // 16) * 8 + (i // 2) * 4 + j % 4
        )
        pick = one_hot(iota((BLK, T), 1) == source)
        perm[i // 2, ds((i % 2) * BLK, BLK), :] = dot(pick, tok[...]).astype(BF16)
        return carry

    lax.fori_loop(0, 4, permute, 0)
    here = ds(g * PIECE, PIECE)
    keeps = [
        pltpu.make_async_copy(perm.at[x, here], arrived.at[i, here], load_sem.at[5 + i])
        for i, x in enumerate((x_lo, 1 - x_lo))
    ]
    for keep in keeps:
        keep.start()

    pl.semaphore_wait(barrier, n_seq - 1 + 4)

    def scatter(i, x):
        def send(k, carry):
            to = (g + k) % groups
            remote(
                perm.at[x, ds(to * PIECE, PIECE)], arrived.at[i, here],
                a2a_s.at[i], a2a_r.at[i], seq=seq_of(to, x_lo),
            ).start()
            return carry

        lax.fori_loop(1, groups, send, 0)

    def rows_to_far(i):
        rows = pl.ds((1 - i) * 2 * BLK, 2 * BLK)
        theirs = row_tok.at[1 - hi, rows, own_lanes]
        return (
            remote(tok.at[rows], row_tok.at[hi, rows, own_lanes], ag_s.at[i], ag_r.at[i], head=far),
            remote(theirs, theirs, ag_s.at[2 + i], ag_r.at[2 + i], head=sib),
        )

    ag_far, ag_fwd = zip(rows_to_far(0), rows_to_far(1))
    ag_sib = remote(tok, row_tok.at[hi, :, own_lanes], ag_s.at[4], ag_r.at[4], head=sib)
    quarter = T // 8
    eighth = quarter // 2

    def wo_quarter(which):
        return w_o.at[ds(far * F + which * quarter, quarter)]

    at = y * quarter + x_lo * eighth
    wo_far = remote(
        wo.at[ds(at, eighth)], w_o.at[ds(h * F + at, eighth)], wo_s.at[0], wo_r.at[0],
        seq=other_seq, head=far,
    )
    wo_sib = remote(wo, w_o.at[ds(h * F, F)], wo_s.at[1], wo_r.at[1], head=sib)
    got = w_o.at[ds(far * F + y * quarter + (1 - x_lo) * eighth, eighth)]
    wo_pair = remote(got, got, wo_s.at[2], wo_r.at[2], seq=other_seq)
    wo_spread = [
        remote(
            wo_quarter(y), wo_quarter(y), wo_s.at[2 + k], wo_r.at[2 + k],
            seq=seq - y + (y + k) % 4,
        )
        for k in range(1, 4)
    ]
    wo_fwd = [
        remote(
            wo_quarter((y - k + 4) % 4), wo_quarter((y - k + 4) % 4),
            wo_s.at[6 + k], wo_r.at[6 + k], head=sib,
        )
        for k in range(4)
    ]

    wo_far.start()
    scatter(0, x_lo)
    ag_far[0].start()
    ag_sib.start()
    scatter(1, 1 - x_lo)
    wo_sib.start()

    def project(source, rows_of, first_row, blocks, write, heads=(0, HEADS)):
        lo, hi_ = heads

        def step(i, carry):
            n, b = i % 3, blocks - 1 - i // 3
            rows = ds(first_row + b * BLK, BLK)
            res = dot(source[rows, :], w_in[n, rows_of, lo * DH : hi_ * DH])
            for k in range(lo, hi_):
                write(n * HEADS + k, rows, res[:, (k - lo) * DH : (k - lo + 1) * DH])
            return carry

        lax.fori_loop(0, 3 * blocks, step, 0)

    def row_first(k, rows, res):
        row_acc[k, rows, :] = res

    def row_last(k, rows, res):
        behind = ds(rows.start + BLK, BLK)
        qkv[k, behind, :] = (row_acc[k, rows, :] + res).astype(BF16)

    def class_first(k, rows, res):
        class_acc[k, rows, :] = res

    def class_last(k, rows, res):
        class_acc[k, rows, :] = class_acc[k, rows, :] + res

    for i in (0, 1, 2, 4):
        loads[i].wait()
    ag_sib.wait_recv()
    project(row_tok.at[hi], own_rows, 0, 4, row_first)

    def mine(x):
        return class_tok.at[hi, ds(x * F, F), own_lanes]

    def theirs(x):
        return class_tok.at[1 - hi, ds(x * F, F), own_lanes]

    to_far = remote(arrived.at[0], mine(x_lo), x_s.at[0], x_r.at[0], head=far)
    to_sib = remote(arrived.at[0], mine(x_lo), x_s.at[1], x_r.at[1], head=sib)
    to_pair = remote(arrived.at[1], mine(x_lo), x_s.at[2], x_r.at[2], seq=other_seq)
    to_cross = remote(
        arrived.at[1], mine(x_lo), x_s.at[3], x_r.at[3], seq=other_seq, head=far
    )
    stay = pltpu.make_async_copy(arrived.at[0], mine(x_lo), load_sem.at[7])

    def forward(i, block):
        return remote(block, block, fwd_s.at[i], fwd_r.at[i], head=sib)

    fwd_far, fwd_pair, fwd_cross = (
        forward(0, theirs(x_lo)), forward(1, mine(1 - x_lo)), forward(2, theirs(1 - x_lo))
    )

    pieces = pl.ds(0, (groups - 1) * PIECE)
    keeps[0].wait()
    wait_for(arrived.at[0, pieces], a2a_r.at[0])
    to_far.start()
    to_sib.start()
    stay.start()

    wo_far.wait_recv()
    wo_pair.start()
    ag_far[0].wait_recv()
    ag_fwd[0].start()
    ag_fwd[0].wait_recv()
    project(row_tok.at[1 - hi], far_rows, 2 * BLK, 2, row_last)
    halo = remote(
        qkv.at[pl.ds(HEADS, 2 * HEADS), pl.ds(T, BLK)],
        qkv.at[pl.ds(HEADS, 2 * HEADS), pl.ds(0, BLK)],
        halo_s.at[0], halo_r.at[0], seq=(seq + 1) % n_seq,
    )
    keeps[1].wait()
    wait_for(arrived.at[1, pieces], a2a_r.at[1])
    to_cross.start()
    to_pair.start()
    halo.start()
    wo_pair.wait_recv()
    for copy in wo_spread:
        copy.start()
    wo_fwd[0].start()

    to_far.wait_recv()
    fwd_far.start()
    to_sib.wait_recv()
    stay.wait()
    project(class_tok.at[hi], own_rows, x_lo * F, 2, class_first)
    fwd_far.wait_recv()
    project(class_tok.at[1 - hi], far_rows, x_lo * F, 2, class_last)

    lower = iota((BLK, BLK), 1) <= iota((BLK, BLK), 0)

    def local(i, carry):
        b = 3 - i
        before = jnp.where(jnp.logical_and(seq == 0, b == 0), NEG, 0.0)
        prev, cur = ds(b * BLK, BLK), ds((b + 1) * BLK, BLK)
        for k in range(HEADS):
            query = qkv[k, cur, :]
            s_cur = dot_t(query, qkv[HEADS + k, cur, :])
            s_prev = dot_t(query, qkv[HEADS + k, prev, :]) + before
            scores = jnp.where(lower, s_cur, s_prev)
            top = jnp.max(scores, axis=1, keepdims=True)
            weights = jnp.exp2((scores - top) * SCALE2)
            total = jnp.sum(weights, axis=1, keepdims=True)
            loc[k, prev, :] = dot(
                jnp.where(lower, weights, 0.0).astype(BF16), qkv[2 * HEADS + k, cur, :]
            ) + dot(
                jnp.where(lower, 0.0, weights).astype(BF16), qkv[2 * HEADS + k, prev, :]
            )
            loc_stat[k, prev, :] = top * SCALE2
            loc_stat[HEADS + k, prev, :] = total
        return carry

    lax.fori_loop(0, 1, local, 0)

    to_pair.wait_recv()
    fwd_pair.start()
    to_cross.wait_recv()
    fwd_cross.start()
    ag_far[1].start()
    fwd_pair.wait_recv()
    project(class_tok.at[hi], own_rows, (1 - x_lo) * F, 2, class_first)
    fwd_cross.wait_recv()

    def row_of(n):
        return ((n % 128) // 16) * 32 + (n // 128) * 16 + n % 16

    earlier = row_of(iota((BLK, BLK), 0)) > row_of(iota((BLK, BLK), 1))
    lane = iota((BLK, DH), 1)
    place = (iota((BLK, DH), 0) % 4) * 32
    slot = g * 2 + x_lo
    own_ret = []
    for pair in range(2):
        heads = (2 * pair, 2 * pair + 2)
        project(class_tok.at[1 - hi], far_rows, (1 - x_lo) * F, 2, class_last, heads)

        def column(k, stat):
            for c in range(4):
                at = pl.ds(c, BLK, stride=4)
                head = 2 * pair + k
                query = class_acc[head, at, :].astype(BF16)
                key = class_acc[HEADS + head, at, :].astype(BF16)
                value = class_acc[2 * HEADS + head, at, :].astype(BF16)
                scores = jnp.where(earlier, dot_t(query, key), NEG)
                top = jnp.max(scores, axis=1, keepdims=True)
                weights = jnp.where(earlier, jnp.exp2((scores - top) * SCALE2), 0.0)
                total = jnp.maximum(jnp.sum(weights, axis=1, keepdims=True), 1.0)
                col_f[k, at, :] = dot(weights.astype(BF16), value) * (1.0 / total)
                level = top * SCALE2 + jnp.log(total) * LOG2E
                stat = jnp.where(lane == place + c * 8 + k, level, stat)
            return stat

        stat = lax.fori_loop(0, 2, column, jnp.zeros((BLK, DH), F32))
        for k in range(2):
            col[pair, :, k * DH : (k + 1) * DH] = col_f[k].astype(BF16)
        gather4 = one_hot(iota((n_seq, BLK), 1) // 4 == iota((n_seq, BLK), 0))
        col_stat[pair, :, 0, :] = select_dot(gather4, stat)

        def copies(to):
            at = ((to // 4) % 2) * groups + (to // 8) * 4 + to % 4
            return (
                (col.at[pair, ds(at * PIECE, PIECE)], ret.at[pair, ds(slot * PIECE, PIECE)]),
                (col_stat.at[pair, at], ret_stat.at[pair, slot]),
            )

        def give_back(k, carry):
            to = (seq + k) % n_seq
            values, stats = copies(to)
            remote(*stats, stat_s.at[pair], stat_r.at[pair], seq=to).start()
            remote(*values, ret_s.at[pair], ret_r.at[pair], seq=to).start()
            return carry

        lax.fori_loop(1, n_seq, give_back, 0)
        for i, (src, dst) in enumerate(copies(seq)):
            own_ret.append(pltpu.make_async_copy(src, dst, load_sem.at[8 + 2 * pair + i]))
            own_ret[-1].start()

    ag_far[1].wait_recv()
    ag_fwd[1].start()
    ag_fwd[1].wait_recv()
    project(row_tok.at[1 - hi], far_rows, 0, 2, row_last)
    for k in range(3):
        wo_spread[k].wait_recv()
        wo_fwd[k + 1].start()
    halo.wait_recv()
    lax.fori_loop(1, 4, local, 0)

    def mix_copy(pair, i, b):
        lanes = pl.ds(pl.multiple_of(core * F + pair * 2 * DH, 2 * DH), 2 * DH)
        return remote(
            send_mix.at[pair, i], mix.at[hi, :, lanes],
            mix_s.at[pair, i], mix_r.at[pair, i], head=b,
        )

    for pair in range(2):
        own_ret[2 * pair].wait()
        own_ret[2 * pair + 1].wait()
        wait_for(ret_stat.at[pair, pl.ds(0, n_seq - 1)], stat_r.at[pair])
        wait_for(ret.at[pair, pl.ds(0, (n_seq - 1) * PIECE)], ret_r.at[pair])
        levels = three_parts(ret_stat[pair, :, 0, :])

        def merge(i, carry):
            b = ((hi + 1 - i // 2) % 2) * 2 + (core + (i + 1) // 2) % 2
            j = iota((BLK, 1), 0)
            pick = one_hot(iota((BLK, T), 1) == (j // 4) * PIECE + b * 4 + j % 4)
            rows = ds(b * BLK, BLK)
            results = dot(pick, ret[pair])
            pick = one_hot(iota((BLK, n_seq), 1) == j // 4)
            spread = sum(dot(pick, part) for part in levels)
            for k in range(2):
                head = 2 * pair + k
                level = jnp.sum(
                    jnp.where(lane == (b * 4 + j % 4) * 8 + k, spread, 0.0),
                    axis=1, keepdims=True,
                )
                top = jnp.maximum(loc_stat[head, rows, :], level)
                local_weight = jnp.exp2(loc_stat[head, rows, :] - top)
                col_weight = jnp.exp2(level - top)
                inv = 1.0 / (loc_stat[HEADS + head, rows, :] * local_weight + col_weight)
                send_mix[pair, i, :, k * DH : (k + 1) * DH] = (
                    loc[head, rows, :] * (local_weight * inv)
                    + results[:, k * DH : (k + 1) * DH] * (col_weight * inv)
                ).astype(BF16)

            @pl.when(i < 3)
            def _():
                mix_copy(pair, i, b).start()

            return carry

        lax.fori_loop(0, 4, merge, 0)
        mix[hi, :, pl.ds(pl.multiple_of(core * F + pair * 2 * DH, 2 * DH), 2 * DH)] = (
            send_mix[pair, 3]
        )

    mix_copies = [
        mix_copy(pair, i, b) for pair in range(2) for i, b in enumerate((far, far_sib, sib))
    ]
    loads[3].wait()
    wo_sib.wait_recv()
    mix_copies[2].wait_recv()
    mix_copies[5].wait_recv()

    def out_first(i, carry):
        res = dot(mix[hi], w_o[own_rows, ds(i * F, F)])
        for k in range(HEADS):
            row_acc[k, ds(i * BLK, BLK), :] = res[:, k * DH : (k + 1) * DH]
        return carry

    lax.fori_loop(0, 4, out_first, 0)
    for copy in wo_fwd:
        copy.wait_recv()
    for i in (0, 1, 3, 4):
        mix_copies[i].wait_recv()

    def out_last(i, carry):
        res = dot(mix[1 - hi], w_o[far_rows, ds(i * F, F)])
        so_far = jnp.concatenate(
            [row_acc[k, ds(i * BLK, BLK), :] for k in range(HEADS)], axis=1
        )
        out[:, ds(i * F, F)] = (res + so_far).astype(BF16)
        return carry

    lax.fori_loop(0, 4, out_last, 0)

    for i in range(2):
        wait_for(perm.at[i, pieces], a2a_s.at[i])
        wait_for(col.at[i, pl.ds(0, (n_seq - 1) * PIECE)], ret_s.at[i])
        wait_for(col_stat.at[i, pl.ds(0, n_seq - 1)], stat_s.at[i])
    for copy in (
        *ag_far, *ag_fwd, ag_sib, to_far, to_sib, to_pair, to_cross,
        fwd_far, fwd_pair, fwd_cross, halo, wo_far, wo_sib, wo_pair, *wo_spread, *wo_fwd,
        *mix_copies,
    ):
        copy.wait_send()


def shards(tokens, w_query, w_key, w_value, w_out):
    vmem = pl.BlockSpec(memory_space=pltpu.VMEM)
    anywhere = pl.BlockSpec(memory_space=pl.ANY)
    dma = lambda n: pltpu.SemaphoreType.DMA((n,))
    d = 4 * F
    n_seq = lax.axis_size("seq")
    return pl.pallas_call(
        kernel,
        out_shape=jax.ShapeDtypeStruct((BLK, d), BF16),
        in_specs=[vmem] + [anywhere] * 4,
        out_specs=vmem,
        scratch_shapes=[
            pltpu.VMEM((2, T, 2 * F), BF16),
            pltpu.VMEM((2, T, 2 * F), BF16),
            pltpu.VMEM((2, T // 2, F), BF16),
            pltpu.VMEM((2, T // 2, F), BF16),
            pltpu.VMEM((3, d, F), BF16),
            pltpu.VMEM((d, d), BF16),
            pltpu.VMEM((12, T, DH), F32),
            pltpu.VMEM((12, T, DH), F32),
            pltpu.VMEM((12, T + BLK, DH), BF16),
            pltpu.VMEM((2, T, DH), F32),
            pltpu.VMEM((2, T, 2 * DH), BF16),
            pltpu.VMEM((2, T, 2 * DH), BF16),
            pltpu.VMEM((2, n_seq, 1, DH), F32),
            pltpu.VMEM((2, n_seq, 1, DH), F32),
            pltpu.VMEM((HEADS, T, DH), F32),
            pltpu.VMEM((2 * HEADS, T, 1), F32),
            pltpu.VMEM((2, 4, BLK, 2 * DH), BF16),
            pltpu.VMEM((2, BLK, 2 * F), BF16),
            dma(12), dma(5), dma(5), dma(2), dma(2), dma(4), dma(4), dma(3), dma(3),
            dma(1), dma(1), dma(2), dma(2), dma(2), dma(2), dma(10), dma(10),
            pltpu.SemaphoreType.DMA((2, 3)), pltpu.SemaphoreType.DMA((2, 3)),
        ],
        compiler_params=pltpu.CompilerParams(
            collective_id=0, has_side_effects=True, vmem_limit_bytes=62 << 20
        ),
    )(tokens, w_query, w_key, w_value, w_out)


def solution(mesh):
    in_specs = (
        P("seq", "head"),
        P(None, "head"),
        P(None, "head"),
        P(None, "head"),
        P("head", None),
    )
    out_specs = P(("seq", "head"), None)
    return jax.shard_map(shards, mesh=mesh, in_specs=in_specs, out_specs=out_specs, check_vma=False)
```

```python
import functools
import math

import jax
import jax.numpy as jnp
from jax import lax
from jax.experimental import pallas as pl
from jax.experimental.pallas import tpu as pltpu
from jax.sharding import PartitionSpec as P

MESH = pl.DeviceIdType.MESH
BF16 = jnp.bfloat16
F32 = jnp.float32
DH = 128
HEADS = 4
T = 1024
F = 512
BLK = 256
PIECE = 16
LOG2E = math.log2(math.e)
SCALE2 = DH ** (-0.5) * LOG2E
NEG = -1e30


def dot(a, b):
    return jnp.dot(a, b, preferred_element_type=F32)


def dot_t(a, b):
    return lax.dot_general(a, b, (((1,), (1,)), ((), ())), preferred_element_type=F32)


def ds(start, size):
    return pl.ds(pl.multiple_of(start, size), size)


def iota(shape, dim):
    return lax.broadcasted_iota(jnp.int32, shape, dim)


def three_parts(value):
    parts = []
    for _ in range(3):
        part = value.astype(BF16)
        parts.append(part)
        value = value - part.astype(F32)
    return parts


def select_dot(pick, value):
    return sum(dot(pick, part) for part in three_parts(value))


def one_hot(hit):
    return jnp.where(hit, 1.0, 0.0).astype(BF16)


def kernel(
    tok, wq, wk, wv, wo, out,
    row_tok, class_tok, perm, arrived, w_in, w_o, row_acc, class_acc, qkv,
    col_f, col, ret, col_stat, ret_stat, loc, loc_stat, send_mix, mix,
    load_sem, ag_s, ag_r, a2a_s, a2a_r, x_s, x_r, fwd_s, fwd_r, halo_s, halo_r,
    ret_s, ret_r, stat_s, stat_r, wo_s, wo_r, mix_s, mix_r,
):
    seq, h = lax.axis_index("seq"), lax.axis_index("head")
    n_seq = lax.axis_size("seq")
    hi, core = h // 2, h % 2
    z, x_lo, y = seq // 8, (seq // 4) % 2, seq % 4
    g = z * 4 + y
    groups = n_seq // 2
    other_seq = z * 8 + (1 - x_lo) * 4 + y
    sib = hi * 2 + 1 - core
    far = (1 - hi) * 2 + core
    far_sib = (1 - hi) * 2 + 1 - core

    def remote(src, dst, s_sem, r_sem, **device):
        return pltpu.make_async_remote_copy(
            src_ref=src, dst_ref=dst, send_sem=s_sem, recv_sem=r_sem,
            device_id=device, device_id_type=MESH,
        )

    def seq_of(group, x):
        return (group // 4) * 8 + x * 4 + group % 4

    def wait_for(ref, sem):
        pltpu.make_async_copy(ref, ref, sem).wait()

    barrier = pltpu.get_barrier_semaphore()

    def greet(k, carry):
        pl.semaphore_signal(
            barrier, inc=1, device_id={"seq": (seq + k) % n_seq}, device_id_type=MESH
        )
        return carry

    lax.fori_loop(1, n_seq, greet, 0)
    for peer in (sib, far, far_sib):
        pl.semaphore_signal(barrier, inc=1, device_id={"head": peer}, device_id_type=MESH)
    pl.semaphore_signal(
        barrier, inc=1, device_id={"seq": other_seq, "head": far}, device_id_type=MESH
    )

    own_lanes = ds(core * F, F)
    own_rows, far_rows = ds(hi * 2 * F, 2 * F), ds((1 - hi) * 2 * F, 2 * F)
    loads = [
        pltpu.make_async_copy(w, w_in.at[i], load_sem.at[i])
        for i, w in enumerate((wq, wk, wv))
    ]
    loads.append(pltpu.make_async_copy(wo, w_o.at[ds(h * F, F)], load_sem.at[3]))
    loads.append(pltpu.make_async_copy(tok, row_tok.at[hi, :, own_lanes], load_sem.at[4]))
    for load in loads:
        load.start()

    def permute(i, carry):
        j = iota((BLK, 1), 0)
        source = (
            ((j // 4) % 4) * BLK + ((i % 2) * 16 + j // 16) * 8 + (i // 2) * 4 + j % 4
        )
        pick = one_hot(iota((BLK, T), 1) == source)
        perm[i // 2, ds((i % 2) * BLK, BLK), :] = dot(pick, tok[...]).astype(BF16)
        return carry

    lax.fori_loop(0, 4, permute, 0)
    here = ds(g * PIECE, PIECE)
    keeps = [
        pltpu.make_async_copy(perm.at[x, here], arrived.at[i, here], load_sem.at[5 + i])
        for i, x in enumerate((x_lo, 1 - x_lo))
    ]
    for keep in keeps:
        keep.start()

    pl.semaphore_wait(barrier, n_seq - 1 + 4)

    def scatter(i, x):
        def send(k, carry):
            to = (g + k) % groups
            remote(
                perm.at[x, ds(to * PIECE, PIECE)], arrived.at[i, here],
                a2a_s.at[i], a2a_r.at[i], seq=seq_of(to, x_lo),
            ).start()
            return carry

        lax.fori_loop(1, groups, send, 0)

    def rows_to_far(i):
        rows = pl.ds(*((3 * BLK, BLK), (2 * BLK, BLK), (0, 2 * BLK))[i])
        theirs = row_tok.at[1 - hi, rows, own_lanes]
        return (
            remote(tok.at[rows], row_tok.at[hi, rows, own_lanes], ag_s.at[i], ag_r.at[i], head=far),
            remote(theirs, theirs, ag_s.at[3 + i], ag_r.at[3 + i], head=sib),
        )

    ag_far, ag_fwd = zip(*(rows_to_far(i) for i in range(3)))
    ag_sib = remote(tok, row_tok.at[hi, :, own_lanes], ag_s.at[6], ag_r.at[6], head=sib)
    quarter = T // 8

    def wo_quarter(which):
        return w_o.at[ds(far * F + which * quarter, quarter)]

    at = y * quarter
    wo_far = remote(
        wo.at[ds(at, quarter)], w_o.at[ds(h * F + at, quarter)], wo_s.at[0], wo_r.at[0],
        seq=other_seq, head=far,
    )
    wo_sib = remote(wo, w_o.at[ds(h * F, F)], wo_s.at[1], wo_r.at[1], head=sib)
    wo_spread = [
        remote(
            wo_quarter(y), wo_quarter(y), wo_s.at[2 + k], wo_r.at[2 + k],
            seq=seq - y + (y + k) % 4,
        )
        for k in range(1, 4)
    ]
    wo_fwd = [
        remote(
            wo_quarter((y - k + 4) % 4), wo_quarter((y - k + 4) % 4),
            wo_s.at[6 + k], wo_r.at[6 + k], head=sib,
        )
        for k in range(4)
    ]

    ag_far[0].start()
    scatter(0, x_lo)
    ag_sib.start()
    ag_far[1].start()
    wo_far.start()
    scatter(1, 1 - x_lo)
    wo_sib.start()

    def project(source, rows_of, first_row, blocks, write, heads=(0, HEADS)):
        lo, hi_ = heads

        def step(i, carry):
            n, b = i % 3, blocks - 1 - i // 3
            rows = ds(first_row + b * BLK, BLK)
            res = dot(source[rows, :], w_in[n, rows_of, lo * DH : hi_ * DH])
            for k in range(lo, hi_):
                write(n * HEADS + k, rows, res[:, (k - lo) * DH : (k - lo + 1) * DH])
            return carry

        lax.fori_loop(0, 3 * blocks, step, 0)

    def row_first(k, rows, res):
        row_acc[k, rows, :] = res

    def row_last(k, rows, res):
        behind = ds(rows.start + BLK, BLK)
        qkv[k, behind, :] = (row_acc[k, rows, :] + res).astype(BF16)

    def class_first(k, rows, res):
        class_acc[k, rows, :] = res

    def class_last(k, rows, res):
        class_acc[k, rows, :] = class_acc[k, rows, :] + res

    for i in (0, 1, 2, 4):
        loads[i].wait()
    ag_sib.wait_recv()
    project(row_tok.at[hi], own_rows, 3 * BLK, 1, row_first)
    ag_far[0].wait_recv()
    ag_fwd[0].start()
    ag_fwd[0].wait_recv()
    project(row_tok.at[1 - hi], far_rows, 3 * BLK, 1, row_last)
    halo = remote(
        qkv.at[pl.ds(HEADS, 2 * HEADS), pl.ds(T, BLK)],
        qkv.at[pl.ds(HEADS, 2 * HEADS), pl.ds(0, BLK)],
        halo_s.at[0], halo_r.at[0], seq=(seq + 1) % n_seq,
    )
    halo.start()
    project(row_tok.at[hi], own_rows, 0, 3, row_first)

    def mine(x):
        return class_tok.at[hi, ds(x * F, F), own_lanes]

    def theirs(x):
        return class_tok.at[1 - hi, ds(x * F, F), own_lanes]

    to_far = remote(arrived.at[0], mine(x_lo), x_s.at[0], x_r.at[0], head=far)
    to_sib = remote(arrived.at[0], mine(x_lo), x_s.at[1], x_r.at[1], head=sib)
    to_pair = remote(arrived.at[1], mine(x_lo), x_s.at[2], x_r.at[2], seq=other_seq)
    to_cross = remote(
        arrived.at[1], mine(x_lo), x_s.at[3], x_r.at[3], seq=other_seq, head=far
    )
    stay = pltpu.make_async_copy(arrived.at[0], mine(x_lo), load_sem.at[7])

    def forward(i, block):
        return remote(block, block, fwd_s.at[i], fwd_r.at[i], head=sib)

    fwd_far, fwd_pair, fwd_cross = (
        forward(0, theirs(x_lo)), forward(1, mine(1 - x_lo)), forward(2, theirs(1 - x_lo))
    )

    pieces = pl.ds(0, (groups - 1) * PIECE)
    keeps[0].wait()
    wait_for(arrived.at[0, pieces], a2a_r.at[0])
    to_far.start()
    to_sib.start()
    stay.start()

    ag_far[1].wait_recv()
    ag_fwd[1].start()
    ag_fwd[1].wait_recv()
    project(row_tok.at[1 - hi], far_rows, 2 * BLK, 1, row_last)
    keeps[1].wait()
    wait_for(arrived.at[1, pieces], a2a_r.at[1])
    to_cross.start()
    to_pair.start()
    wo_far.wait_recv()
    for copy in wo_spread:
        copy.start()
    wo_fwd[0].start()

    to_far.wait_recv()
    fwd_far.start()
    to_sib.wait_recv()
    stay.wait()
    project(class_tok.at[hi], own_rows, x_lo * F, 2, class_first)
    fwd_far.wait_recv()
    project(class_tok.at[1 - hi], far_rows, x_lo * F, 2, class_last)

    lower = iota((BLK, BLK), 1) <= iota((BLK, BLK), 0)

    def local(i, carry):
        b = 3 - i
        before = jnp.where(jnp.logical_and(seq == 0, b == 0), NEG, 0.0)
        prev, cur = ds(b * BLK, BLK), ds((b + 1) * BLK, BLK)
        for k in range(HEADS):
            query = qkv[k, cur, :]
            s_cur = dot_t(query, qkv[HEADS + k, cur, :])
            s_prev = dot_t(query, qkv[HEADS + k, prev, :]) + before
            scores = jnp.where(lower, s_cur, s_prev)
            top = jnp.max(scores, axis=1, keepdims=True)
            weights = jnp.exp2((scores - top) * SCALE2)
            total = jnp.sum(weights, axis=1, keepdims=True)
            loc[k, prev, :] = dot(
                jnp.where(lower, weights, 0.0).astype(BF16), qkv[2 * HEADS + k, cur, :]
            ) + dot(
                jnp.where(lower, 0.0, weights).astype(BF16), qkv[2 * HEADS + k, prev, :]
            )
            loc_stat[k, prev, :] = top * SCALE2
            loc_stat[HEADS + k, prev, :] = total
        return carry

    lax.fori_loop(0, 1, local, 0)

    to_pair.wait_recv()
    fwd_pair.start()
    to_cross.wait_recv()
    fwd_cross.start()
    ag_far[2].start()
    fwd_pair.wait_recv()
    project(class_tok.at[hi], own_rows, (1 - x_lo) * F, 2, class_first)
    fwd_cross.wait_recv()

    def row_of(n):
        return ((n % 128) // 16) * 32 + (n // 128) * 16 + n % 16

    earlier = row_of(iota((BLK, BLK), 0)) > row_of(iota((BLK, BLK), 1))
    lane = iota((BLK, DH), 1)
    place = (iota((BLK, DH), 0) % 4) * 32
    slot = g * 2 + x_lo
    own_ret = []
    for pair in range(2):
        heads = (2 * pair, 2 * pair + 2)
        project(class_tok.at[1 - hi], far_rows, (1 - x_lo) * F, 2, class_last, heads)

        def column(k, stat):
            for c in range(4):
                at = pl.ds(c, BLK, stride=4)
                head = 2 * pair + k
                query = class_acc[head, at, :].astype(BF16)
                key = class_acc[HEADS + head, at, :].astype(BF16)
                value = class_acc[2 * HEADS + head, at, :].astype(BF16)
                scores = jnp.where(earlier, dot_t(query, key), NEG)
                top = jnp.max(scores, axis=1, keepdims=True)
                weights = jnp.where(earlier, jnp.exp2((scores - top) * SCALE2), 0.0)
                total = jnp.maximum(jnp.sum(weights, axis=1, keepdims=True), 1.0)
                col_f[k, at, :] = dot(weights.astype(BF16), value) * (1.0 / total)
                level = top * SCALE2 + jnp.log(total) * LOG2E
                stat = jnp.where(lane == place + c * 8 + k, level, stat)
            return stat

        stat = lax.fori_loop(0, 2, column, jnp.zeros((BLK, DH), F32))
        for k in range(2):
            col[pair, :, k * DH : (k + 1) * DH] = col_f[k].astype(BF16)
        gather4 = one_hot(iota((n_seq, BLK), 1) // 4 == iota((n_seq, BLK), 0))
        col_stat[pair, :, 0, :] = select_dot(gather4, stat)

        def copies(to):
            at = ((to // 4) % 2) * groups + (to // 8) * 4 + to % 4
            return (
                (col.at[pair, ds(at * PIECE, PIECE)], ret.at[pair, ds(slot * PIECE, PIECE)]),
                (col_stat.at[pair, at], ret_stat.at[pair, slot]),
            )

        def give_back(k, carry):
            to = (seq + k) % n_seq
            values, stats = copies(to)
            remote(*stats, stat_s.at[pair], stat_r.at[pair], seq=to).start()
            remote(*values, ret_s.at[pair], ret_r.at[pair], seq=to).start()
            return carry

        lax.fori_loop(1, n_seq, give_back, 0)
        for i, (src, dst) in enumerate(copies(seq)):
            own_ret.append(pltpu.make_async_copy(src, dst, load_sem.at[8 + 2 * pair + i]))
            own_ret[-1].start()

    ag_far[2].wait_recv()
    ag_fwd[2].start()
    ag_fwd[2].wait_recv()
    project(row_tok.at[1 - hi], far_rows, 0, 2, row_last)
    for k in range(3):
        wo_spread[k].wait_recv()
        wo_fwd[k + 1].start()
    halo.wait_recv()
    lax.fori_loop(1, 4, local, 0)

    def mix_copy(pair, i, b):
        lanes = pl.ds(pl.multiple_of(core * F + pair * 2 * DH, 2 * DH), 2 * DH)
        return remote(
            send_mix.at[pair, i], mix.at[hi, :, lanes],
            mix_s.at[pair, i], mix_r.at[pair, i], head=b,
        )

    for pair in range(2):
        own_ret[2 * pair].wait()
        own_ret[2 * pair + 1].wait()
        wait_for(ret_stat.at[pair, pl.ds(0, n_seq - 1)], stat_r.at[pair])
        wait_for(ret.at[pair, pl.ds(0, (n_seq - 1) * PIECE)], ret_r.at[pair])
        levels = three_parts(ret_stat[pair, :, 0, :])

        def merge(i, carry):
            b = ((hi + 1 - i // 2) % 2) * 2 + (core + (i + 1) // 2) % 2
            j = iota((BLK, 1), 0)
            pick = one_hot(iota((BLK, T), 1) == (j // 4) * PIECE + b * 4 + j % 4)
            rows = ds(b * BLK, BLK)
            results = dot(pick, ret[pair])
            pick = one_hot(iota((BLK, n_seq), 1) == j // 4)
            spread = sum(dot(pick, part) for part in levels)
            for k in range(2):
                head = 2 * pair + k
                level = jnp.sum(
                    jnp.where(lane == (b * 4 + j % 4) * 8 + k, spread, 0.0),
                    axis=1, keepdims=True,
                )
                top = jnp.maximum(loc_stat[head, rows, :], level)
                local_weight = jnp.exp2(loc_stat[head, rows, :] - top)
                col_weight = jnp.exp2(level - top)
                inv = 1.0 / (loc_stat[HEADS + head, rows, :] * local_weight + col_weight)
                send_mix[pair, i, :, k * DH : (k + 1) * DH] = (
                    loc[head, rows, :] * (local_weight * inv)
                    + results[:, k * DH : (k + 1) * DH] * (col_weight * inv)
                ).astype(BF16)

            @pl.when(i < 3)
            def _():
                mix_copy(pair, i, b).start()

            return carry

        lax.fori_loop(0, 4, merge, 0)
        mix[hi, :, pl.ds(pl.multiple_of(core * F + pair * 2 * DH, 2 * DH), 2 * DH)] = (
            send_mix[pair, 3]
        )

    mix_copies = [
        mix_copy(pair, i, b) for pair in range(2) for i, b in enumerate((far, far_sib, sib))
    ]
    loads[3].wait()
    wo_sib.wait_recv()
    mix_copies[2].wait_recv()
    mix_copies[5].wait_recv()

    def out_first(i, carry):
        res = dot(mix[hi], w_o[own_rows, ds(i * F, F)])
        for k in range(HEADS):
            row_acc[k, ds(i * BLK, BLK), :] = res[:, k * DH : (k + 1) * DH]
        return carry

    lax.fori_loop(0, 4, out_first, 0)
    for copy in wo_fwd:
        copy.wait_recv()
    for i in (0, 1, 3, 4):
        mix_copies[i].wait_recv()

    def out_last(i, carry):
        res = dot(mix[1 - hi], w_o[far_rows, ds(i * F, F)])
        so_far = jnp.concatenate(
            [row_acc[k, ds(i * BLK, BLK), :] for k in range(HEADS)], axis=1
        )
        out[:, ds(i * F, F)] = (res + so_far).astype(BF16)
        return carry

    lax.fori_loop(0, 4, out_last, 0)

    for i in range(2):
        wait_for(perm.at[i, pieces], a2a_s.at[i])
        wait_for(col.at[i, pl.ds(0, (n_seq - 1) * PIECE)], ret_s.at[i])
        wait_for(col_stat.at[i, pl.ds(0, n_seq - 1)], stat_s.at[i])
    for copy in (
        *ag_far, *ag_fwd, ag_sib, to_far, to_sib, to_pair, to_cross,
        fwd_far, fwd_pair, fwd_cross, halo, wo_far, wo_sib, *wo_spread, *wo_fwd,
        *mix_copies,
    ):
        copy.wait_send()


def shards(tokens, w_query, w_key, w_value, w_out):
    vmem = pl.BlockSpec(memory_space=pltpu.VMEM)
    anywhere = pl.BlockSpec(memory_space=pl.ANY)
    dma = lambda n: pltpu.SemaphoreType.DMA((n,))
    d = 4 * F
    n_seq = lax.axis_size("seq")
    return pl.pallas_call(
        kernel,
        out_shape=jax.ShapeDtypeStruct((BLK, d), BF16),
        in_specs=[vmem] + [anywhere] * 4,
        out_specs=vmem,
        scratch_shapes=[
            pltpu.VMEM((2, T, 2 * F), BF16),
            pltpu.VMEM((2, T, 2 * F), BF16),
            pltpu.VMEM((2, T // 2, F), BF16),
            pltpu.VMEM((2, T // 2, F), BF16),
            pltpu.VMEM((3, d, F), BF16),
            pltpu.VMEM((d, d), BF16),
            pltpu.VMEM((12, T, DH), F32),
            pltpu.VMEM((12, T, DH), F32),
            pltpu.VMEM((12, T + BLK, DH), BF16),
            pltpu.VMEM((2, T, DH), F32),
            pltpu.VMEM((2, T, 2 * DH), BF16),
            pltpu.VMEM((2, T, 2 * DH), BF16),
            pltpu.VMEM((2, n_seq, 1, DH), F32),
            pltpu.VMEM((2, n_seq, 1, DH), F32),
            pltpu.VMEM((HEADS, T, DH), F32),
            pltpu.VMEM((2 * HEADS, T, 1), F32),
            pltpu.VMEM((2, 4, BLK, 2 * DH), BF16),
            pltpu.VMEM((2, BLK, 2 * F), BF16),
            dma(12), dma(7), dma(7), dma(2), dma(2), dma(4), dma(4), dma(3), dma(3),
            dma(1), dma(1), dma(2), dma(2), dma(2), dma(2), dma(10), dma(10),
            pltpu.SemaphoreType.DMA((2, 3)), pltpu.SemaphoreType.DMA((2, 3)),
        ],
        compiler_params=pltpu.CompilerParams(
            collective_id=0, has_side_effects=True, vmem_limit_bytes=62 << 20
        ),
    )(tokens, w_query, w_key, w_value, w_out)


def solution(mesh):
    in_specs = (
        P("seq", "head"),
        P(None, "head"),
        P(None, "head"),
        P(None, "head"),
        P("head", None),
    )
    out_specs = P(("seq", "head"), None)
    return jax.shard_map(shards, mesh=mesh, in_specs=in_specs, out_specs=out_specs, check_vma=False)
```

```python
import functools
import math

import jax
import jax.numpy as jnp
from jax import lax
from jax.experimental import pallas as pl
from jax.experimental.pallas import tpu as pltpu
from jax.sharding import PartitionSpec as P

MESH = pl.DeviceIdType.MESH
BF16 = jnp.bfloat16
F32 = jnp.float32
DH = 128
HEADS = 4
T = 1024
F = 512
BLK = 256
PIECE = 16
LOG2E = math.log2(math.e)
SCALE2 = DH ** (-0.5) * LOG2E
NEG = -1e30


def dot(a, b):
    return jnp.dot(a, b, preferred_element_type=F32)


def dot_t(a, b):
    return lax.dot_general(a, b, (((1,), (1,)), ((), ())), preferred_element_type=F32)


def ds(start, size):
    return pl.ds(pl.multiple_of(start, size), size)


def iota(shape, dim):
    return lax.broadcasted_iota(jnp.int32, shape, dim)


def three_parts(value):
    parts = []
    for _ in range(3):
        part = value.astype(BF16)
        parts.append(part)
        value = value - part.astype(F32)
    return parts


def select_dot(pick, value):
    return sum(dot(pick, part) for part in three_parts(value))


def one_hot(hit):
    return jnp.where(hit, 1.0, 0.0).astype(BF16)


def kernel(
    tok, wq, wk, wv, wo, out,
    row_tok, class_tok, perm, arrived, w_in, w_o, row_acc, class_acc, qkv,
    col_f, col, ret, col_stat, ret_stat, loc, loc_stat, send_mix, mix,
    load_sem, ag_s, ag_r, a2a_s, a2a_r, x_s, x_r, fwd_s, fwd_r, halo_s, halo_r,
    ret_s, ret_r, stat_s, stat_r, wo_s, wo_r, mix_s, mix_r,
):
    seq, h = lax.axis_index("seq"), lax.axis_index("head")
    n_seq = lax.axis_size("seq")
    hi, core = h // 2, h % 2
    z, x_lo, y = seq // 8, (seq // 4) % 2, seq % 4
    g = z * 4 + y
    groups = n_seq // 2
    other_seq = z * 8 + (1 - x_lo) * 4 + y
    sib = hi * 2 + 1 - core
    far = (1 - hi) * 2 + core
    far_sib = (1 - hi) * 2 + 1 - core

    def remote(src, dst, s_sem, r_sem, **device):
        return pltpu.make_async_remote_copy(
            src_ref=src, dst_ref=dst, send_sem=s_sem, recv_sem=r_sem,
            device_id=device, device_id_type=MESH,
        )

    def seq_of(group, x):
        return (group // 4) * 8 + x * 4 + group % 4

    def wait_for(ref, sem):
        pltpu.make_async_copy(ref, ref, sem).wait()

    barrier = pltpu.get_barrier_semaphore()

    def greet(k, carry):
        pl.semaphore_signal(
            barrier, inc=1, device_id={"seq": (seq + k) % n_seq}, device_id_type=MESH
        )
        return carry

    lax.fori_loop(1, n_seq, greet, 0)
    for peer in (sib, far, far_sib):
        pl.semaphore_signal(barrier, inc=1, device_id={"head": peer}, device_id_type=MESH)
    pl.semaphore_signal(
        barrier, inc=1, device_id={"seq": other_seq, "head": far}, device_id_type=MESH
    )

    own_lanes = ds(core * F, F)
    own_rows, far_rows = ds(hi * 2 * F, 2 * F), ds((1 - hi) * 2 * F, 2 * F)
    loads = [
        pltpu.make_async_copy(w, w_in.at[i], load_sem.at[i])
        for i, w in enumerate((wq, wk, wv))
    ]
    loads.append(pltpu.make_async_copy(wo, w_o.at[ds(h * F, F)], load_sem.at[3]))
    loads.append(pltpu.make_async_copy(tok, row_tok.at[hi, :, own_lanes], load_sem.at[4]))
    for load in loads:
        load.start()

    def permute(i, carry):
        j = iota((BLK, 1), 0)
        source = (
            ((j // 4) % 4) * BLK + ((i % 2) * 16 + j // 16) * 8 + (i // 2) * 4 + j % 4
        )
        pick = one_hot(iota((BLK, T), 1) == source)
        perm[i // 2, ds((i % 2) * BLK, BLK), :] = dot(pick, tok[...]).astype(BF16)
        return carry

    lax.fori_loop(0, 4, permute, 0)
    here = ds(g * PIECE, PIECE)
    keeps = [
        pltpu.make_async_copy(perm.at[x, here], arrived.at[i, here], load_sem.at[5 + i])
        for i, x in enumerate((x_lo, 1 - x_lo))
    ]
    for keep in keeps:
        keep.start()

    pl.semaphore_wait(barrier, n_seq - 1 + 4)

    def scatter(i, x):
        def send(k, carry):
            to = (g + k) % groups
            remote(
                perm.at[x, ds(to * PIECE, PIECE)], arrived.at[i, here],
                a2a_s.at[i], a2a_r.at[i], seq=seq_of(to, x_lo),
            ).start()
            return carry

        lax.fori_loop(1, groups, send, 0)

    def rows_to_far(i):
        rows = pl.ds(*((3 * BLK, BLK), (2 * BLK, BLK), (0, 2 * BLK))[i])
        theirs = row_tok.at[1 - hi, rows, own_lanes]
        return (
            remote(tok.at[rows], row_tok.at[hi, rows, own_lanes], ag_s.at[i], ag_r.at[i], head=far),
            remote(theirs, theirs, ag_s.at[3 + i], ag_r.at[3 + i], head=sib),
        )

    ag_far, ag_fwd = zip(*(rows_to_far(i) for i in range(3)))
    ag_sib = remote(tok, row_tok.at[hi, :, own_lanes], ag_s.at[6], ag_r.at[6], head=sib)
    quarter = T // 8

    def wo_quarter(which):
        return w_o.at[ds(far * F + which * quarter, quarter)]

    at = y * quarter
    wo_far = remote(
        wo.at[ds(at, quarter)], w_o.at[ds(h * F + at, quarter)], wo_s.at[0], wo_r.at[0],
        seq=other_seq, head=far,
    )
    wo_sib = remote(wo, w_o.at[ds(h * F, F)], wo_s.at[1], wo_r.at[1], head=sib)
    wo_spread = [
        remote(
            wo_quarter(y), wo_quarter(y), wo_s.at[2 + k], wo_r.at[2 + k],
            seq=seq - y + (y + k) % 4,
        )
        for k in range(1, 4)
    ]
    wo_fwd = [
        remote(
            wo_quarter((y - k + 4) % 4), wo_quarter((y - k + 4) % 4),
            wo_s.at[6 + k], wo_r.at[6 + k], head=sib,
        )
        for k in range(4)
    ]

    ag_far[0].start()
    scatter(0, x_lo)
    ag_sib.start()
    ag_far[1].start()
    wo_far.start()
    scatter(1, 1 - x_lo)
    wo_sib.start()

    def project(source, rows_of, first_row, blocks, write, heads=(0, HEADS)):
        lo, hi_ = heads

        def step(i, carry):
            n, b = i % 3, blocks - 1 - i // 3
            rows = ds(first_row + b * BLK, BLK)
            res = dot(source[rows, :], w_in[n, rows_of, lo * DH : hi_ * DH])
            for k in range(lo, hi_):
                write(n * HEADS + k, rows, res[:, (k - lo) * DH : (k - lo + 1) * DH])
            return carry

        lax.fori_loop(0, 3 * blocks, step, 0)

    def row_first(k, rows, res):
        row_acc[k, rows, :] = res

    def row_last(k, rows, res):
        behind = ds(rows.start + BLK, BLK)
        qkv[k, behind, :] = (row_acc[k, rows, :] + res).astype(BF16)

    def class_first(k, rows, res):
        class_acc[k, rows, :] = res

    def class_last(k, rows, res):
        class_acc[k, rows, :] = class_acc[k, rows, :] + res

    for i in (0, 1, 2, 4):
        loads[i].wait()
    ag_sib.wait_recv()
    project(row_tok.at[hi], own_rows, 3 * BLK, 1, row_first)
    ag_far[0].wait_recv()
    ag_fwd[0].start()
    ag_fwd[0].wait_recv()
    project(row_tok.at[1 - hi], far_rows, 3 * BLK, 1, row_last)
    halo = remote(
        qkv.at[pl.ds(HEADS, 2 * HEADS), pl.ds(T, BLK)],
        qkv.at[pl.ds(HEADS, 2 * HEADS), pl.ds(0, BLK)],
        halo_s.at[0], halo_r.at[0], seq=(seq + 1) % n_seq,
    )
    halo.start()
    project(row_tok.at[hi], own_rows, 0, 3, row_first)

    def mine(x):
        return class_tok.at[hi, ds(x * F, F), own_lanes]

    def theirs(x):
        return class_tok.at[1 - hi, ds(x * F, F), own_lanes]

    to_far = remote(arrived.at[0], mine(x_lo), x_s.at[0], x_r.at[0], head=far)
    to_sib = remote(arrived.at[0], mine(x_lo), x_s.at[1], x_r.at[1], head=sib)
    def part(i):
        return pl.ds(i * BLK, BLK)

    def place(c, x, i):
        return class_tok.at[c, ds(x * F + i * BLK, BLK), own_lanes]

    to_pair = [
        remote(
            arrived.at[1, part(i)], place(hi, x_lo, i), x_s.at[2 + i], x_r.at[2 + i],
            seq=other_seq,
        )
        for i in range(2)
    ]
    to_cross = [
        remote(
            arrived.at[1, part(i)], place(hi, x_lo, i), x_s.at[4 + i], x_r.at[4 + i],
            seq=other_seq, head=far,
        )
        for i in range(2)
    ]
    stay = pltpu.make_async_copy(arrived.at[0], mine(x_lo), load_sem.at[7])

    def forward(i, block):
        return remote(block, block, fwd_s.at[i], fwd_r.at[i], head=sib)

    fwd_far = forward(0, theirs(x_lo))
    fwd_pair = [forward(1 + i, place(hi, 1 - x_lo, i)) for i in range(2)]
    fwd_cross = [forward(3 + i, place(1 - hi, 1 - x_lo, i)) for i in range(2)]

    pieces = pl.ds(0, (groups - 1) * PIECE)
    keeps[0].wait()
    wait_for(arrived.at[0, pieces], a2a_r.at[0])
    to_far.start()
    to_sib.start()
    stay.start()

    ag_far[1].wait_recv()
    ag_fwd[1].start()
    ag_fwd[1].wait_recv()
    project(row_tok.at[1 - hi], far_rows, 2 * BLK, 1, row_last)
    keeps[1].wait()
    wait_for(arrived.at[1, pieces], a2a_r.at[1])
    for i in range(2):
        to_cross[i].start()
        to_pair[i].start()
    wo_far.wait_recv()
    for copy in wo_spread:
        copy.start()
    wo_fwd[0].start()

    to_far.wait_recv()
    fwd_far.start()
    to_sib.wait_recv()
    stay.wait()
    project(class_tok.at[hi], own_rows, x_lo * F, 2, class_first)
    fwd_far.wait_recv()
    project(class_tok.at[1 - hi], far_rows, x_lo * F, 2, class_last)

    lower = iota((BLK, BLK), 1) <= iota((BLK, BLK), 0)

    def local(i, carry):
        b = 3 - i
        before = jnp.where(jnp.logical_and(seq == 0, b == 0), NEG, 0.0)
        prev, cur = ds(b * BLK, BLK), ds((b + 1) * BLK, BLK)
        for k in range(HEADS):
            query = qkv[k, cur, :]
            s_cur = dot_t(query, qkv[HEADS + k, cur, :])
            s_prev = dot_t(query, qkv[HEADS + k, prev, :]) + before
            scores = jnp.where(lower, s_cur, s_prev)
            top = jnp.max(scores, axis=1, keepdims=True)
            weights = jnp.exp2((scores - top) * SCALE2)
            total = jnp.sum(weights, axis=1, keepdims=True)
            loc[k, prev, :] = dot(
                jnp.where(lower, weights, 0.0).astype(BF16), qkv[2 * HEADS + k, cur, :]
            ) + dot(
                jnp.where(lower, 0.0, weights).astype(BF16), qkv[2 * HEADS + k, prev, :]
            )
            loc_stat[k, prev, :] = top * SCALE2
            loc_stat[HEADS + k, prev, :] = total
        return carry

    lax.fori_loop(0, 1, local, 0)

    def from_x(i):
        to_pair[i].wait_recv()
        fwd_pair[i].start()
        to_cross[i].wait_recv()
        fwd_cross[i].start()

    def from_sib(i):
        fwd_pair[i].wait_recv()
        project(class_tok.at[hi], own_rows, (1 - x_lo) * F + i * BLK, 1, class_first)
        fwd_cross[i].wait_recv()

    from_x(0)
    from_sib(0)
    project(class_tok.at[1 - hi], far_rows, (1 - x_lo) * F, 1, class_last)
    from_x(1)
    ag_far[2].start()
    from_sib(1)

    def row_of(n):
        return ((n % 128) // 16) * 32 + (n // 128) * 16 + n % 16

    earlier = row_of(iota((BLK, BLK), 0)) > row_of(iota((BLK, BLK), 1))
    lane = iota((BLK, DH), 1)
    place = (iota((BLK, DH), 0) % 4) * 32
    slot = g * 2 + x_lo
    own_ret = []
    for pair in range(2):
        heads = (2 * pair, 2 * pair + 2)
        project(class_tok.at[1 - hi], far_rows, (1 - x_lo) * F + BLK, 1, class_last, heads)

        def column(k, stat):
            for c in range(4):
                at = pl.ds(c, BLK, stride=4)
                head = 2 * pair + k
                query = class_acc[head, at, :].astype(BF16)
                key = class_acc[HEADS + head, at, :].astype(BF16)
                value = class_acc[2 * HEADS + head, at, :].astype(BF16)
                scores = jnp.where(earlier, dot_t(query, key), NEG)
                top = jnp.max(scores, axis=1, keepdims=True)
                weights = jnp.where(earlier, jnp.exp2((scores - top) * SCALE2), 0.0)
                total = jnp.maximum(jnp.sum(weights, axis=1, keepdims=True), 1.0)
                col_f[k, at, :] = dot(weights.astype(BF16), value) * (1.0 / total)
                level = top * SCALE2 + jnp.log(total) * LOG2E
                stat = jnp.where(lane == place + c * 8 + k, level, stat)
            return stat

        stat = lax.fori_loop(0, 2, column, jnp.zeros((BLK, DH), F32))
        for k in range(2):
            col[pair, :, k * DH : (k + 1) * DH] = col_f[k].astype(BF16)
        gather4 = one_hot(iota((n_seq, BLK), 1) // 4 == iota((n_seq, BLK), 0))
        col_stat[pair, :, 0, :] = select_dot(gather4, stat)

        def copies(to):
            at = ((to // 4) % 2) * groups + (to // 8) * 4 + to % 4
            return (
                (col.at[pair, ds(at * PIECE, PIECE)], ret.at[pair, ds(slot * PIECE, PIECE)]),
                (col_stat.at[pair, at], ret_stat.at[pair, slot]),
            )

        def give_back(k, carry):
            to = (seq + k) % n_seq
            values, stats = copies(to)
            remote(*stats, stat_s.at[pair], stat_r.at[pair], seq=to).start()
            remote(*values, ret_s.at[pair], ret_r.at[pair], seq=to).start()
            return carry

        lax.fori_loop(1, n_seq, give_back, 0)
        for i, (src, dst) in enumerate(copies(seq)):
            own_ret.append(pltpu.make_async_copy(src, dst, load_sem.at[8 + 2 * pair + i]))
            own_ret[-1].start()

    ag_far[2].wait_recv()
    ag_fwd[2].start()
    ag_fwd[2].wait_recv()
    project(row_tok.at[1 - hi], far_rows, 0, 2, row_last)
    for k in range(3):
        wo_spread[k].wait_recv()
        wo_fwd[k + 1].start()
    halo.wait_recv()
    lax.fori_loop(1, 4, local, 0)

    def mix_copy(pair, i, b):
        lanes = pl.ds(pl.multiple_of(core * F + pair * 2 * DH, 2 * DH), 2 * DH)
        return remote(
            send_mix.at[pair, i], mix.at[hi, :, lanes],
            mix_s.at[pair, i], mix_r.at[pair, i], head=b,
        )

    for pair in range(2):
        own_ret[2 * pair].wait()
        own_ret[2 * pair + 1].wait()
        wait_for(ret_stat.at[pair, pl.ds(0, n_seq - 1)], stat_r.at[pair])
        wait_for(ret.at[pair, pl.ds(0, (n_seq - 1) * PIECE)], ret_r.at[pair])
        levels = three_parts(ret_stat[pair, :, 0, :])

        def merge(i, carry):
            b = ((hi + 1 - i // 2) % 2) * 2 + (core + (i + 1) // 2) % 2
            j = iota((BLK, 1), 0)
            pick = one_hot(iota((BLK, T), 1) == (j // 4) * PIECE + b * 4 + j % 4)
            rows = ds(b * BLK, BLK)
            results = dot(pick, ret[pair])
            pick = one_hot(iota((BLK, n_seq), 1) == j // 4)
            spread = sum(dot(pick, part) for part in levels)
            for k in range(2):
                head = 2 * pair + k
                level = jnp.sum(
                    jnp.where(lane == (b * 4 + j % 4) * 8 + k, spread, 0.0),
                    axis=1, keepdims=True,
                )
                top = jnp.maximum(loc_stat[head, rows, :], level)
                local_weight = jnp.exp2(loc_stat[head, rows, :] - top)
                col_weight = jnp.exp2(level - top)
                inv = 1.0 / (loc_stat[HEADS + head, rows, :] * local_weight + col_weight)
                send_mix[pair, i, :, k * DH : (k + 1) * DH] = (
                    loc[head, rows, :] * (local_weight * inv)
                    + results[:, k * DH : (k + 1) * DH] * (col_weight * inv)
                ).astype(BF16)

            @pl.when(i < 3)
            def _():
                mix_copy(pair, i, b).start()

            return carry

        lax.fori_loop(0, 4, merge, 0)
        mix[hi, :, pl.ds(pl.multiple_of(core * F + pair * 2 * DH, 2 * DH), 2 * DH)] = (
            send_mix[pair, 3]
        )

    mix_copies = [
        mix_copy(pair, i, b) for pair in range(2) for i, b in enumerate((far, far_sib, sib))
    ]
    loads[3].wait()
    wo_sib.wait_recv()
    mix_copies[2].wait_recv()
    mix_copies[5].wait_recv()

    def out_first(i, carry):
        res = dot(mix[hi], w_o[own_rows, ds(i * F, F)])
        for k in range(HEADS):
            row_acc[k, ds(i * BLK, BLK), :] = res[:, k * DH : (k + 1) * DH]
        return carry

    lax.fori_loop(0, 4, out_first, 0)
    for copy in wo_fwd:
        copy.wait_recv()
    for i in (0, 1, 3, 4):
        mix_copies[i].wait_recv()

    def out_last(i, carry):
        res = dot(mix[1 - hi], w_o[far_rows, ds(i * F, F)])
        so_far = jnp.concatenate(
            [row_acc[k, ds(i * BLK, BLK), :] for k in range(HEADS)], axis=1
        )
        out[:, ds(i * F, F)] = (res + so_far).astype(BF16)
        return carry

    lax.fori_loop(0, 4, out_last, 0)

    for i in range(2):
        wait_for(perm.at[i, pieces], a2a_s.at[i])
        wait_for(col.at[i, pl.ds(0, (n_seq - 1) * PIECE)], ret_s.at[i])
        wait_for(col_stat.at[i, pl.ds(0, n_seq - 1)], stat_s.at[i])
    for copy in (
        *ag_far, *ag_fwd, ag_sib, to_far, to_sib, *to_pair, *to_cross,
        fwd_far, *fwd_pair, *fwd_cross, halo, wo_far, wo_sib, *wo_spread, *wo_fwd,
        *mix_copies,
    ):
        copy.wait_send()


def shards(tokens, w_query, w_key, w_value, w_out):
    vmem = pl.BlockSpec(memory_space=pltpu.VMEM)
    anywhere = pl.BlockSpec(memory_space=pl.ANY)
    dma = lambda n: pltpu.SemaphoreType.DMA((n,))
    d = 4 * F
    n_seq = lax.axis_size("seq")
    return pl.pallas_call(
        kernel,
        out_shape=jax.ShapeDtypeStruct((BLK, d), BF16),
        in_specs=[vmem] + [anywhere] * 4,
        out_specs=vmem,
        scratch_shapes=[
            pltpu.VMEM((2, T, 2 * F), BF16),
            pltpu.VMEM((2, T, 2 * F), BF16),
            pltpu.VMEM((2, T // 2, F), BF16),
            pltpu.VMEM((2, T // 2, F), BF16),
            pltpu.VMEM((3, d, F), BF16),
            pltpu.VMEM((d, d), BF16),
            pltpu.VMEM((12, T, DH), F32),
            pltpu.VMEM((12, T, DH), F32),
            pltpu.VMEM((12, T + BLK, DH), BF16),
            pltpu.VMEM((2, T, DH), F32),
            pltpu.VMEM((2, T, 2 * DH), BF16),
            pltpu.VMEM((2, T, 2 * DH), BF16),
            pltpu.VMEM((2, n_seq, 1, DH), F32),
            pltpu.VMEM((2, n_seq, 1, DH), F32),
            pltpu.VMEM((HEADS, T, DH), F32),
            pltpu.VMEM((2 * HEADS, T, 1), F32),
            pltpu.VMEM((2, 4, BLK, 2 * DH), BF16),
            pltpu.VMEM((2, BLK, 2 * F), BF16),
            dma(12), dma(7), dma(7), dma(2), dma(2), dma(6), dma(6), dma(5), dma(5),
            dma(1), dma(1), dma(2), dma(2), dma(2), dma(2), dma(10), dma(10),
            pltpu.SemaphoreType.DMA((2, 3)), pltpu.SemaphoreType.DMA((2, 3)),
        ],
        compiler_params=pltpu.CompilerParams(
            collective_id=0, has_side_effects=True, vmem_limit_bytes=62 << 20
        ),
    )(tokens, w_query, w_key, w_value, w_out)


def solution(mesh):
    in_specs = (
        P("seq", "head"),
        P(None, "head"),
        P(None, "head"),
        P(None, "head"),
        P("head", None),
    )
    out_specs = P(("seq", "head"), None)
    return jax.shard_map(shards, mesh=mesh, in_specs=in_specs, out_specs=out_specs, check_vma=False)
```

```python
import functools
import math

import jax
import jax.numpy as jnp
from jax import lax
from jax.experimental import pallas as pl
from jax.experimental.pallas import tpu as pltpu
from jax.sharding import PartitionSpec as P

MESH = pl.DeviceIdType.MESH
BF16 = jnp.bfloat16
F32 = jnp.float32
DH = 128
HEADS = 4
T = 1024
F = 512
BLK = 256
PIECE = 16
LOG2E = math.log2(math.e)
SCALE2 = DH ** (-0.5) * LOG2E
NEG = -1e30


def dot(a, b):
    return jnp.dot(a, b, preferred_element_type=F32)


def dot_t(a, b):
    return lax.dot_general(a, b, (((1,), (1,)), ((), ())), preferred_element_type=F32)


def ds(start, size):
    return pl.ds(pl.multiple_of(start, size), size)


def iota(shape, dim):
    return lax.broadcasted_iota(jnp.int32, shape, dim)


def three_parts(value):
    parts = []
    for _ in range(3):
        part = value.astype(BF16)
        parts.append(part)
        value = value - part.astype(F32)
    return parts


def select_dot(pick, value):
    return sum(dot(pick, part) for part in three_parts(value))


def one_hot(hit):
    return jnp.where(hit, 1.0, 0.0).astype(BF16)


def kernel(
    tok, wq, wk, wv, wo, out,
    row_tok, class_tok, perm, arrived, w_in, w_o, row_acc, class_acc, qkv,
    col_f, col, ret, col_stat, ret_stat, loc, loc_stat, send_mix, mix,
    load_sem, ag_s, ag_r, a2a_s, a2a_r, x_s, x_r, fwd_s, fwd_r, halo_s, halo_r,
    ret_s, ret_r, stat_s, stat_r, wo_s, wo_r, mix_s, mix_r,
):
    seq, h = lax.axis_index("seq"), lax.axis_index("head")
    n_seq = lax.axis_size("seq")
    hi, core = h // 2, h % 2
    z, x_lo, y = seq // 8, (seq // 4) % 2, seq % 4
    g = z * 4 + y
    groups = n_seq // 2
    other_seq = z * 8 + (1 - x_lo) * 4 + y
    sib = hi * 2 + 1 - core
    far = (1 - hi) * 2 + core
    far_sib = (1 - hi) * 2 + 1 - core

    def remote(src, dst, s_sem, r_sem, **device):
        return pltpu.make_async_remote_copy(
            src_ref=src, dst_ref=dst, send_sem=s_sem, recv_sem=r_sem,
            device_id=device, device_id_type=MESH,
        )

    def seq_of(group, x):
        return (group // 4) * 8 + x * 4 + group % 4

    def wait_for(ref, sem):
        pltpu.make_async_copy(ref, ref, sem).wait()

    barrier = pltpu.get_barrier_semaphore()

    def greet(k, carry):
        pl.semaphore_signal(
            barrier, inc=1, device_id={"seq": (seq + k) % n_seq}, device_id_type=MESH
        )
        return carry

    lax.fori_loop(1, n_seq, greet, 0)
    for peer in (sib, far, far_sib):
        pl.semaphore_signal(barrier, inc=1, device_id={"head": peer}, device_id_type=MESH)
    pl.semaphore_signal(
        barrier, inc=1, device_id={"seq": other_seq, "head": far}, device_id_type=MESH
    )

    own_lanes = ds(core * F, F)
    own_rows, far_rows = ds(hi * 2 * F, 2 * F), ds((1 - hi) * 2 * F, 2 * F)
    loads = [
        pltpu.make_async_copy(w, w_in.at[i], load_sem.at[i])
        for i, w in enumerate((wq, wk, wv))
    ]
    loads.append(pltpu.make_async_copy(wo, w_o.at[ds(h * F, F)], load_sem.at[3]))
    loads.append(pltpu.make_async_copy(tok, row_tok.at[hi, :, own_lanes], load_sem.at[4]))
    for load in loads:
        load.start()

    def permute(i, carry):
        j = iota((BLK, 1), 0)
        source = (
            ((j // 4) % 4) * BLK + ((i % 2) * 16 + j // 16) * 8 + (i // 2) * 4 + j % 4
        )
        pick = one_hot(iota((BLK, T), 1) == source)
        perm[i // 2, ds((i % 2) * BLK, BLK), :] = dot(pick, tok[...]).astype(BF16)
        return carry

    lax.fori_loop(0, 4, permute, 0)
    here = ds(g * PIECE, PIECE)
    keeps = [
        pltpu.make_async_copy(perm.at[x, here], arrived.at[i, here], load_sem.at[5 + i])
        for i, x in enumerate((x_lo, 1 - x_lo))
    ]
    for keep in keeps:
        keep.start()

    pl.semaphore_wait(barrier, n_seq - 1 + 4)

    def scatter(i, x):
        def send(k, carry):
            to = (g + k) % groups
            remote(
                perm.at[x, ds(to * PIECE, PIECE)], arrived.at[i, here],
                a2a_s.at[i], a2a_r.at[i], seq=seq_of(to, x_lo),
            ).start()
            return carry

        lax.fori_loop(1, groups, send, 0)

    def rows_to_far(i):
        rows = pl.ds(*((3 * BLK, BLK), (2 * BLK, BLK), (0, 2 * BLK))[i])
        theirs = row_tok.at[1 - hi, rows, own_lanes]
        return (
            remote(tok.at[rows], row_tok.at[hi, rows, own_lanes], ag_s.at[i], ag_r.at[i], head=far),
            remote(theirs, theirs, ag_s.at[3 + i], ag_r.at[3 + i], head=sib),
        )

    ag_far, ag_fwd = zip(*(rows_to_far(i) for i in range(3)))
    ag_sib = remote(tok, row_tok.at[hi, :, own_lanes], ag_s.at[6], ag_r.at[6], head=sib)
    quarter = T // 8

    def wo_quarter(which):
        return w_o.at[ds(far * F + which * quarter, quarter)]

    at = y * quarter
    wo_far = remote(
        wo.at[ds(at, quarter)], w_o.at[ds(h * F + at, quarter)], wo_s.at[0], wo_r.at[0],
        seq=other_seq, head=far,
    )
    wo_sib = remote(wo, w_o.at[ds(h * F, F)], wo_s.at[1], wo_r.at[1], head=sib)
    wo_spread = [
        remote(
            wo_quarter(y), wo_quarter(y), wo_s.at[2 + k], wo_r.at[2 + k],
            seq=seq - y + (y + k) % 4,
        )
        for k in range(1, 4)
    ]
    wo_fwd = [
        remote(
            wo_quarter((y - k + 4) % 4), wo_quarter((y - k + 4) % 4),
            wo_s.at[6 + k], wo_r.at[6 + k], head=sib,
        )
        for k in range(4)
    ]

    ag_far[0].start()
    scatter(0, x_lo)
    ag_sib.start()
    ag_far[1].start()
    scatter(1, 1 - x_lo)
    wo_sib.start()

    def project(source, rows_of, first_row, blocks, write, heads=(0, HEADS)):
        lo, hi_ = heads

        def step(i, carry):
            n, b = i % 3, blocks - 1 - i // 3
            rows = ds(first_row + b * BLK, BLK)
            res = dot(source[rows, :], w_in[n, rows_of, lo * DH : hi_ * DH])
            for k in range(lo, hi_):
                write(n * HEADS + k, rows, res[:, (k - lo) * DH : (k - lo + 1) * DH])
            return carry

        lax.fori_loop(0, 3 * blocks, step, 0)

    def row_first(k, rows, res):
        row_acc[k, rows, :] = res

    def row_last(k, rows, res):
        behind = ds(rows.start + BLK, BLK)
        qkv[k, behind, :] = (row_acc[k, rows, :] + res).astype(BF16)

    def class_first(k, rows, res):
        class_acc[k, rows, :] = res

    def class_last(k, rows, res):
        class_acc[k, rows, :] = class_acc[k, rows, :] + res

    for i in (0, 1, 2, 4):
        loads[i].wait()
    ag_sib.wait_recv()
    project(row_tok.at[hi], own_rows, 3 * BLK, 1, row_first)
    ag_far[0].wait_recv()
    ag_fwd[0].start()
    ag_fwd[0].wait_recv()
    project(row_tok.at[1 - hi], far_rows, 3 * BLK, 1, row_last)
    halo = remote(
        qkv.at[pl.ds(HEADS, 2 * HEADS), pl.ds(T, BLK)],
        qkv.at[pl.ds(HEADS, 2 * HEADS), pl.ds(0, BLK)],
        halo_s.at[0], halo_r.at[0], seq=(seq + 1) % n_seq,
    )
    halo.start()
    wo_far.start()
    project(row_tok.at[hi], own_rows, 0, 3, row_first)

    def mine(x):
        return class_tok.at[hi, ds(x * F, F), own_lanes]

    def theirs(x):
        return class_tok.at[1 - hi, ds(x * F, F), own_lanes]

    to_far = remote(arrived.at[0], mine(x_lo), x_s.at[0], x_r.at[0], head=far)
    to_sib = remote(arrived.at[0], mine(x_lo), x_s.at[1], x_r.at[1], head=sib)
    def part(i):
        return pl.ds(i * BLK, BLK)

    def place(c, x, i):
        return class_tok.at[c, ds(x * F + i * BLK, BLK), own_lanes]

    to_pair = [
        remote(
            arrived.at[1, part(i)], place(hi, x_lo, i), x_s.at[2 + i], x_r.at[2 + i],
            seq=other_seq,
        )
        for i in range(2)
    ]
    to_cross = [
        remote(
            arrived.at[1, part(i)], place(hi, x_lo, i), x_s.at[4 + i], x_r.at[4 + i],
            seq=other_seq, head=far,
        )
        for i in range(2)
    ]
    stay = pltpu.make_async_copy(arrived.at[0], mine(x_lo), load_sem.at[7])

    def forward(i, block):
        return remote(block, block, fwd_s.at[i], fwd_r.at[i], head=sib)

    fwd_far = forward(0, theirs(x_lo))
    fwd_pair = [forward(1 + i, place(hi, 1 - x_lo, i)) for i in range(2)]
    fwd_cross = [forward(3 + i, place(1 - hi, 1 - x_lo, i)) for i in range(2)]

    pieces = pl.ds(0, (groups - 1) * PIECE)
    keeps[0].wait()
    wait_for(arrived.at[0, pieces], a2a_r.at[0])
    to_far.start()
    to_sib.start()
    stay.start()

    ag_far[1].wait_recv()
    ag_fwd[1].start()
    ag_fwd[1].wait_recv()
    project(row_tok.at[1 - hi], far_rows, 2 * BLK, 1, row_last)
    keeps[1].wait()
    wait_for(arrived.at[1, pieces], a2a_r.at[1])
    for i in range(2):
        to_cross[i].start()
        to_pair[i].start()
    wo_far.wait_recv()
    for copy in wo_spread:
        copy.start()
    wo_fwd[0].start()

    to_far.wait_recv()
    fwd_far.start()
    to_sib.wait_recv()
    stay.wait()
    project(class_tok.at[hi], own_rows, x_lo * F, 2, class_first)
    fwd_far.wait_recv()
    project(class_tok.at[1 - hi], far_rows, x_lo * F, 2, class_last)

    lower = iota((BLK, BLK), 1) <= iota((BLK, BLK), 0)

    def local(i, carry):
        b = 3 - i
        before = jnp.where(jnp.logical_and(seq == 0, b == 0), NEG, 0.0)
        prev, cur = ds(b * BLK, BLK), ds((b + 1) * BLK, BLK)
        for k in range(HEADS):
            query = qkv[k, cur, :]
            s_cur = dot_t(query, qkv[HEADS + k, cur, :])
            s_prev = dot_t(query, qkv[HEADS + k, prev, :]) + before
            scores = jnp.where(lower, s_cur, s_prev)
            top = jnp.max(scores, axis=1, keepdims=True)
            weights = jnp.exp2((scores - top) * SCALE2)
            total = jnp.sum(weights, axis=1, keepdims=True)
            loc[k, prev, :] = dot(
                jnp.where(lower, weights, 0.0).astype(BF16), qkv[2 * HEADS + k, cur, :]
            ) + dot(
                jnp.where(lower, 0.0, weights).astype(BF16), qkv[2 * HEADS + k, prev, :]
            )
            loc_stat[k, prev, :] = top * SCALE2
            loc_stat[HEADS + k, prev, :] = total
        return carry

    lax.fori_loop(0, 1, local, 0)

    def from_x(i):
        to_pair[i].wait_recv()
        fwd_pair[i].start()
        to_cross[i].wait_recv()
        fwd_cross[i].start()

    def from_sib(i):
        fwd_pair[i].wait_recv()
        project(class_tok.at[hi], own_rows, (1 - x_lo) * F + i * BLK, 1, class_first)
        fwd_cross[i].wait_recv()

    from_x(0)
    from_sib(0)
    project(class_tok.at[1 - hi], far_rows, (1 - x_lo) * F, 1, class_last)
    from_x(1)
    ag_far[2].start()
    from_sib(1)

    def row_of(n):
        return ((n % 128) // 16) * 32 + (n // 128) * 16 + n % 16

    earlier = row_of(iota((BLK, BLK), 0)) > row_of(iota((BLK, BLK), 1))
    lane = iota((BLK, DH), 1)
    place = (iota((BLK, DH), 0) % 4) * 32
    slot = g * 2 + x_lo
    own_ret = []
    for pair in range(2):
        heads = (2 * pair, 2 * pair + 2)
        project(class_tok.at[1 - hi], far_rows, (1 - x_lo) * F + BLK, 1, class_last, heads)

        def column(k, stat):
            for c in range(4):
                at = pl.ds(c, BLK, stride=4)
                head = 2 * pair + k
                query = class_acc[head, at, :].astype(BF16)
                key = class_acc[HEADS + head, at, :].astype(BF16)
                value = class_acc[2 * HEADS + head, at, :].astype(BF16)
                scores = jnp.where(earlier, dot_t(query, key), NEG)
                top = jnp.max(scores, axis=1, keepdims=True)
                weights = jnp.where(earlier, jnp.exp2((scores - top) * SCALE2), 0.0)
                total = jnp.maximum(jnp.sum(weights, axis=1, keepdims=True), 1.0)
                col_f[k, at, :] = dot(weights.astype(BF16), value) * (1.0 / total)
                level = top * SCALE2 + jnp.log(total) * LOG2E
                stat = jnp.where(lane == place + c * 8 + k, level, stat)
            return stat

        stat = lax.fori_loop(0, 2, column, jnp.zeros((BLK, DH), F32))
        for k in range(2):
            col[pair, :, k * DH : (k + 1) * DH] = col_f[k].astype(BF16)
        gather4 = one_hot(iota((n_seq, BLK), 1) // 4 == iota((n_seq, BLK), 0))
        col_stat[pair, :, 0, :] = select_dot(gather4, stat)

        def copies(to):
            at = ((to // 4) % 2) * groups + (to // 8) * 4 + to % 4
            return (
                (col.at[pair, ds(at * PIECE, PIECE)], ret.at[pair, ds(slot * PIECE, PIECE)]),
                (col_stat.at[pair, at], ret_stat.at[pair, slot]),
            )

        def give_back(k, carry):
            to = (seq + k) % n_seq
            values, stats = copies(to)
            remote(*stats, stat_s.at[pair], stat_r.at[pair], seq=to).start()
            remote(*values, ret_s.at[pair], ret_r.at[pair], seq=to).start()
            return carry

        lax.fori_loop(1, n_seq, give_back, 0)
        for i, (src, dst) in enumerate(copies(seq)):
            own_ret.append(pltpu.make_async_copy(src, dst, load_sem.at[8 + 2 * pair + i]))
            own_ret[-1].start()

    ag_far[2].wait_recv()
    ag_fwd[2].start()
    ag_fwd[2].wait_recv()
    project(row_tok.at[1 - hi], far_rows, 0, 2, row_last)
    for k in range(3):
        wo_spread[k].wait_recv()
        wo_fwd[k + 1].start()
    halo.wait_recv()
    lax.fori_loop(1, 4, local, 0)

    def mix_copy(pair, i, b):
        lanes = pl.ds(pl.multiple_of(core * F + pair * 2 * DH, 2 * DH), 2 * DH)
        return remote(
            send_mix.at[pair, i], mix.at[hi, :, lanes],
            mix_s.at[pair, i], mix_r.at[pair, i], head=b,
        )

    for pair in range(2):
        own_ret[2 * pair].wait()
        own_ret[2 * pair + 1].wait()
        wait_for(ret_stat.at[pair, pl.ds(0, n_seq - 1)], stat_r.at[pair])
        wait_for(ret.at[pair, pl.ds(0, (n_seq - 1) * PIECE)], ret_r.at[pair])
        levels = three_parts(ret_stat[pair, :, 0, :])

        def merge(i, carry):
            b = ((hi + 1 - i // 2) % 2) * 2 + (core + (i + 1) // 2) % 2
            j = iota((BLK, 1), 0)
            pick = one_hot(iota((BLK, T), 1) == (j // 4) * PIECE + b * 4 + j % 4)
            rows = ds(b * BLK, BLK)
            results = dot(pick, ret[pair])
            pick = one_hot(iota((BLK, n_seq), 1) == j // 4)
            spread = sum(dot(pick, part) for part in levels)
            for k in range(2):
                head = 2 * pair + k
                level = jnp.sum(
                    jnp.where(lane == (b * 4 + j % 4) * 8 + k, spread, 0.0),
                    axis=1, keepdims=True,
                )
                top = jnp.maximum(loc_stat[head, rows, :], level)
                local_weight = jnp.exp2(loc_stat[head, rows, :] - top)
                col_weight = jnp.exp2(level - top)
                inv = 1.0 / (loc_stat[HEADS + head, rows, :] * local_weight + col_weight)
                send_mix[pair, i, :, k * DH : (k + 1) * DH] = (
                    loc[head, rows, :] * (local_weight * inv)
                    + results[:, k * DH : (k + 1) * DH] * (col_weight * inv)
                ).astype(BF16)

            @pl.when(i < 3)
            def _():
                mix_copy(pair, i, b).start()

            return carry

        lax.fori_loop(0, 4, merge, 0)
        mix[hi, :, pl.ds(pl.multiple_of(core * F + pair * 2 * DH, 2 * DH), 2 * DH)] = (
            send_mix[pair, 3]
        )

    mix_copies = [
        mix_copy(pair, i, b) for pair in range(2) for i, b in enumerate((far, far_sib, sib))
    ]
    loads[3].wait()
    wo_sib.wait_recv()
    mix_copies[2].wait_recv()
    mix_copies[5].wait_recv()

    def out_first(i, carry):
        res = dot(mix[hi], w_o[own_rows, ds(i * F, F)])
        for k in range(HEADS):
            row_acc[k, ds(i * BLK, BLK), :] = res[:, k * DH : (k + 1) * DH]
        return carry

    lax.fori_loop(0, 4, out_first, 0)
    for copy in wo_fwd:
        copy.wait_recv()
    for i in (0, 1, 3, 4):
        mix_copies[i].wait_recv()

    def out_last(i, carry):
        res = dot(mix[1 - hi], w_o[far_rows, ds(i * F, F)])
        so_far = jnp.concatenate(
            [row_acc[k, ds(i * BLK, BLK), :] for k in range(HEADS)], axis=1
        )
        out[:, ds(i * F, F)] = (res + so_far).astype(BF16)
        return carry

    lax.fori_loop(0, 4, out_last, 0)

    for i in range(2):
        wait_for(perm.at[i, pieces], a2a_s.at[i])
        wait_for(col.at[i, pl.ds(0, (n_seq - 1) * PIECE)], ret_s.at[i])
        wait_for(col_stat.at[i, pl.ds(0, n_seq - 1)], stat_s.at[i])
    for copy in (
        *ag_far, *ag_fwd, ag_sib, to_far, to_sib, *to_pair, *to_cross,
        fwd_far, *fwd_pair, *fwd_cross, halo, wo_far, wo_sib, *wo_spread, *wo_fwd,
        *mix_copies,
    ):
        copy.wait_send()


def shards(tokens, w_query, w_key, w_value, w_out):
    vmem = pl.BlockSpec(memory_space=pltpu.VMEM)
    anywhere = pl.BlockSpec(memory_space=pl.ANY)
    dma = lambda n: pltpu.SemaphoreType.DMA((n,))
    d = 4 * F
    n_seq = lax.axis_size("seq")
    return pl.pallas_call(
        kernel,
        out_shape=jax.ShapeDtypeStruct((BLK, d), BF16),
        in_specs=[vmem] + [anywhere] * 4,
        out_specs=vmem,
        scratch_shapes=[
            pltpu.VMEM((2, T, 2 * F), BF16),
            pltpu.VMEM((2, T, 2 * F), BF16),
            pltpu.VMEM((2, T // 2, F), BF16),
            pltpu.VMEM((2, T // 2, F), BF16),
            pltpu.VMEM((3, d, F), BF16),
            pltpu.VMEM((d, d), BF16),
            pltpu.VMEM((12, T, DH), F32),
            pltpu.VMEM((12, T, DH), F32),
            pltpu.VMEM((12, T + BLK, DH), BF16),
            pltpu.VMEM((2, T, DH), F32),
            pltpu.VMEM((2, T, 2 * DH), BF16),
            pltpu.VMEM((2, T, 2 * DH), BF16),
            pltpu.VMEM((2, n_seq, 1, DH), F32),
            pltpu.VMEM((2, n_seq, 1, DH), F32),
            pltpu.VMEM((HEADS, T, DH), F32),
            pltpu.VMEM((2 * HEADS, T, 1), F32),
            pltpu.VMEM((2, 4, BLK, 2 * DH), BF16),
            pltpu.VMEM((2, BLK, 2 * F), BF16),
            dma(12), dma(7), dma(7), dma(2), dma(2), dma(6), dma(6), dma(5), dma(5),
            dma(1), dma(1), dma(2), dma(2), dma(2), dma(2), dma(10), dma(10),
            pltpu.SemaphoreType.DMA((2, 3)), pltpu.SemaphoreType.DMA((2, 3)),
        ],
        compiler_params=pltpu.CompilerParams(
            collective_id=0, has_side_effects=True, vmem_limit_bytes=62 << 20
        ),
    )(tokens, w_query, w_key, w_value, w_out)


def solution(mesh):
    in_specs = (
        P("seq", "head"),
        P(None, "head"),
        P(None, "head"),
        P(None, "head"),
        P("head", None),
    )
    out_specs = P(("seq", "head"), None)
    return jax.shard_map(shards, mesh=mesh, in_specs=in_specs, out_specs=out_specs, check_vma=False)
```
